128 devices in a mesh: vel: 8 (over y, z_lo), space: 16 (over x, z_hi, core).
Axes of the slice: x: 4, y: 4, z: 4 (z_hi: 2, z_lo: 2; z = z_hi * 2 + z_lo), core: 2. Of those that a mesh axis runs over, the one named last changes fastest.
Arguments:
- density: float32 [1024, 64, 8, 128], P('vel', 'space'), may hold values from -6 to 6
- limiter: int32 [64, 8, 128], P('space'), may hold values from 0 to 2
- heading: int32 [1024], P('vel'), may hold values from 0 to 1
- courant: float32 [1024], P('vel'), may hold values from 0.1 to 0.9
- kernel_slices: bfloat16 [16, 1024, 1024], P('space', None, 'vel'), may hold values from -0.046875 to 0.046875
Outputs:
- transported: float32 [1024, 64, 8, 128], P('vel', 'space')
- collision: float32 [1024, 64, 8, 128], P('vel', 'space')
The draws below stay inside these ranges and needn't reach their ends.
Inputs may be any that keep to these rules, and one draw needn't show every extreme that they name: `limiter`: 0 no slope, 1 minmod slope, 2 central slope.
All inputs are finite; a program needn't handle non-finite values.
Results may differ from the reference program's by a relative error of at most 0.0041.
Values may be sent and summed in bfloat16 or wider, within the bound.
No kernel may reach another device: no remote copies, remote signals or barrier semaphores. Data moves between devices by JAX's collectives and lax.ppermute only.
A program may use at most 128 MiB of HBM per device.

```python
import math
import jax
import jax.numpy as jnp
from jax import lax

V = 1024
SLICES = 16
NY = 8
NZ = 128
NX = 64


def touch_ends(result, key, smallest, high):
    shape = result.shape
    spot = [jax.random.randint(jax.random.fold_in(key, axis), (), 0, shape[axis]) for axis in range(len(shape))]
    result = result.at[tuple(spot)].set(smallest)
    longest = shape.index(max(shape))
    spot[longest] = (spot[longest] + 1) % shape[longest]
    return result.at[tuple(spot)].set(high)


def levels(stream_key, shape, split, smallest, top_value):
    loudness = 1.0
    for dim, blocks in split:
        heights = jax.random.uniform(jax.random.fold_in(jax.random.fold_in(stream_key, 6), dim), (blocks,), jnp.float32, smallest / len(split), top_value / len(split))
        loudness = loudness * jnp.repeat(jnp.exp(heights), shape[dim] // blocks).reshape((-1,) + (1,) * (len(shape) - 1 - dim))
    return loudness


def scatter_about(key, shape, scale, limit, split=(), kind=jnp.bfloat16):
    factor_of = levels(key, shape, split, -0.22, 0.18) if split else 1.0
    values = jax.random.normal(key, shape, jnp.float32) * scale * factor_of
    return jnp.minimum(jnp.maximum(values, -limit), limit).astype(kind)


def setup_inputs(seed: int = 0) -> dict:
    key_list = jax.random.split(jax.random.key(seed), 6)
    density = scatter_about(key_list[0], (V, NX, NY, NZ), 1.0, 6.0, ((0, 8), (1, 16)), jnp.float32)
    limiter = touch_ends(jax.random.randint(key_list[1], (NX, NY, NZ), 0, 3), jax.random.fold_in(key_list[1], 1), 0, 2).astype(jnp.int32)
    heading = touch_ends(jax.random.randint(key_list[2], (V,), 0, 2), jax.random.fold_in(key_list[2], 1), 0, 1).astype(jnp.int32)
    courant = jnp.clip(jnp.exp(math.log(0.9) - 2.1972245 * jax.random.uniform(key_list[3], (V,), jnp.float32) ** levels(key_list[3], (V,), ((0, 8),), -0.2, 0.2)), 0.1, 0.9)
    kernel_slices = scatter_about(key_list[4], (SLICES, V, V), (V * SLICES) ** -0.5, 0.046875, ((0, 16), (2, 8)))
    return dict(density=density, limiter=limiter, heading=heading, courant=courant, kernel_slices=kernel_slices)


def limited_slopes(left_diff, right_diff, limiter):
    minmod_slope = jnp.where(left_diff * right_diff > 0, jnp.sign(left_diff) * jnp.minimum(jnp.abs(left_diff), jnp.abs(right_diff)), jnp.zeros_like(left_diff))
    central = 0.5 * (left_diff + right_diff)
    codes = limiter[None]
    return jnp.where(codes == 1, minmod_slope, jnp.where(codes == 2, central, jnp.zeros_like(central)))


def reference(density, limiter, heading, courant, kernel_slices):
    layers = ((0, 0), (1, 1), (0, 0), (0, 0))
    padded = jnp.pad(density, layers)
    left_diff = density - padded[:, :-2]
    right_diff = padded[:, 2:] - density
    slopes = limited_slopes(left_diff, right_diff, limiter)
    upwind = (2 * heading - 1).astype(density.dtype)[:, None, None, None]
    rebuilt = density + 0.5 * upwind * slopes
    rebuilt_pad = jnp.pad(rebuilt, layers)
    forward = (heading == 1)[:, None, None, None]
    upstream = jnp.where(forward, rebuilt_pad[:, :-2], rebuilt_pad[:, 2:])
    transported = density - courant[:, None, None, None] * (rebuilt - upstream)
    moved = transported.astype(jnp.bfloat16).reshape(V, -1)
    stride = V // SLICES

    def apply_one(running, position):
        matrix = kernel_slices[position]
        projected = jnp.dot(matrix.T, moved, preferred_element_type=jnp.float32)
        weight = moved[position * stride].astype(jnp.float32)
        return running + weight[None, :] * projected, position

    initial = jnp.zeros(moved.shape, jnp.float32)
    collision = lax.scan(apply_one, initial, jnp.arange(SLICES, dtype=jnp.int32))[0]
    return transported, collision.reshape(density.shape)
```

```python
import jax
import jax.numpy as jnp
from jax import lax
from jax.experimental import pallas as pl
from jax.experimental.pallas import tpu as pltpu
from jax.sharding import PartitionSpec as P

SLICES = 16
LAYERS = 4
BOTH = ("vel", "space")
FLAT = [
    (y, z, x, h, c)
    for y in range(4)
    for z in range(2)
    for x in range(4)
    for h in range(2)
    for c in range(2)
]


def rank(y, z, x, h, c):
    return ((y % 4) * 2 + z) * 16 + (x % 4) * 4 + h * 2 + c


def shift(value, dy=0, dz=0, dx=0, dh=0, dc=0):
    pairs = [
        (rank(y, z, x, h, c), rank(y + dy, z ^ dz, x + dx, h ^ dh, c ^ dc)) for y, z, x, h, c in FLAT
    ]
    return lax.ppermute(value, BOTH, pairs)


def halos(density, limiter):
    codes = limiter.astype(jnp.bfloat16)[None]
    upper = jnp.concatenate([density[:, 2:].astype(jnp.bfloat16), codes[:, 2:]], 0)
    lower = jnp.concatenate([density[:, :2].astype(jnp.bfloat16), codes[:, :2]], 0)
    size = lax.axis_size("space")
    up = [(i, i + 1) for i in range(size - 1)]
    below = lax.ppermute(upper, "space", up)
    above = lax.ppermute(lower, "space", [(j, i) for i, j in up])
    return below, above


def transport(density, limiter, heading, courant, below, above):
    rows = density.shape[0]
    f32 = jnp.float32
    padded = jnp.concatenate([below[:rows].astype(f32), density, above[:rows].astype(f32)], 1)
    codes = jnp.concatenate(
        [below[rows:, 1:], limiter[None].astype(jnp.bfloat16), above[rows:, :1]], 1
    ).astype(f32)
    middle = padded[:, 1:-1]
    left = middle - padded[:, :-2]
    right = padded[:, 2:] - middle
    minmod = jnp.where(
        left * right > 0, jnp.sign(left) * jnp.minimum(jnp.abs(left), jnp.abs(right)), 0.0
    )
    slope = jnp.where(codes == 1, minmod, jnp.where(codes == 2, 0.5 * (left + right), 0.0))
    upwind = (2 * heading - 1).astype(f32)[:, None, None, None]
    rebuilt = middle + 0.5 * upwind * slope
    forward = (heading == 1)[:, None, None, None]
    upstream = jnp.where(forward, rebuilt[:, :-2], rebuilt[:, 2:])
    return density - courant[:, None, None, None] * (rebuilt[:, 1:-1] - upstream)


def gather_slices(kernel_slices):
    z = lax.axis_index("vel") % 2
    own = kernel_slices[0].reshape(4, 2, 128, 128)
    keep = lax.dynamic_index_in_dim(own, z, 1, keepdims=False).reshape(512, 128).T
    send = lax.dynamic_index_in_dim(own, 1 - z, 1, keepdims=False).reshape(512, 128).T
    here = shift(send, dz=1)
    far = shift(keep, dh=1)
    cross = shift(send, dz=1, dh=1)
    base = jnp.concatenate([keep, here, far, cross], 0)
    one = shift(base, dx=1)
    three = shift(base, dx=-1)
    two_a = shift(one[:512 // 2], dx=1)
    two_b = shift(three[512 // 2 :], dx=-1)
    pieces = [base, one, three, two_a, two_b]
    return pieces + [shift(p, dc=1) for p in pieces]


ORDER = [(0, 0), (0, 1), (3, 0), (3, 1), (1, 0), (1, 1), (2, 0), (2, 1)]


def weight_rows():
    vel, space = lax.axis_index("vel"), lax.axis_index("space")
    y, z = vel // 2, vel % 2
    x, h, c = space // 4, (space // 2) % 2, space % 2
    rows = []
    for dc in range(2):
        for dx, dh in ORDER:
            s = ((x + dx) % 4) * 4 + (h ^ dh) * 2 + (c ^ dc)
            v = s // 2
            rows.append(((v // 2 - y) % 4) * 4 + ((v % 2) ^ z) * 2 + s % 2)
    return jnp.stack(rows + [y] + [y] * 15).astype(jnp.int32)


def collide(table, pieces, blocks, weights):
    cells = blocks[0].shape[1]
    tile = 512

    def kernel(table_ref, w_ref, *refs):
        slabs = refs[:10]
        parts = refs[10:14]
        mine_ref, other_ref, k_ref, m_ref, sem_k, sem_m = refs[14:]
        y = table_ref[SLICES]
        loads = []
        for d in range(4):
            at = pl.multiple_of(((y + d) % 4) * 128, 128)
            loads.append(pltpu.make_async_copy(parts[d], m_ref.at[pl.ds(at, 128)], sem_m.at[d]))
        row, starts = 0, []
        for i in range(10):
            n = slabs[i].shape[0]
            loads.append(
                pltpu.make_async_copy(slabs[i], k_ref.at[pl.ds(row, n)], sem_k.at[i])
            )
            starts.append(row // 256)
            row += n
        for load in loads:
            load.start()
        for load in loads[:4]:
            load.wait()
        for t in range(cells // tile):
            cols = pl.ds(t * tile, tile)
            moved = m_ref[:, cols]
            total = jnp.zeros((256, tile), jnp.float32)
            for s in range(SLICES):
                if t == 0 and s in starts:
                    loads[4 + starts.index(s)].wait()
                product = jnp.dot(
                    k_ref[s * 256 : (s + 1) * 256], moved, preferred_element_type=jnp.float32
                )
                total = total + w_ref[pl.ds(table_ref[s], 1), cols] * product
            mine_ref[:, cols] = total[:128]
            other_ref[:, cols] = total[128:].astype(jnp.bfloat16)

    anywhere = pl.BlockSpec(memory_space=pl.ANY)
    vmem = pl.BlockSpec(memory_space=pltpu.VMEM)
    return pl.pallas_call(
        kernel,
        out_shape=(
            jax.ShapeDtypeStruct((128, cells), jnp.float32),
            jax.ShapeDtypeStruct((128, cells), jnp.bfloat16),
        ),
        in_specs=[pl.BlockSpec(memory_space=pltpu.SMEM), vmem] + [anywhere] * 14,
        out_specs=(vmem, vmem),
        scratch_shapes=[
            pltpu.VMEM((SLICES * 256, 512), jnp.bfloat16),
            pltpu.VMEM((512, cells), jnp.bfloat16),
            pltpu.SemaphoreType.DMA((10,)),
            pltpu.SemaphoreType.DMA((4,)),
        ],
        compiler_params=pltpu.CompilerParams(vmem_limit_bytes=24 << 20),
        cost_estimate=pl.CostEstimate(
            flops=2 * SLICES * 256 * 512 * cells, bytes_accessed=6 << 20, transcendentals=0
        ),
        name="collide",
    )(table, weights, *pieces, *blocks)


def local(density, limiter, heading, courant, kernel_slices):
    below, above = halos(density, limiter)
    pieces = gather_slices(kernel_slices)
    transported = transport(density, limiter, heading, courant, below, above)
    cells = density.shape[2] * density.shape[3]
    moved = transported.astype(jnp.bfloat16)
    chunks = [moved[:, i].reshape(-1, cells) for i in range(LAYERS)]
    own = moved.reshape(2, 64, -1)[:, 0]
    rows = jnp.concatenate([own, shift(own, dz=1)], 0)
    weights = jnp.concatenate(
        [rows, shift(rows, dy=-1), shift(rows, dy=2), shift(rows, dy=1)], 0
    ).astype(jnp.float32)
    table = weight_rows()
    results = []
    for i, block in enumerate(chunks):
        before = shift(block, dy=1)
        after = shift(block, dy=-1)
        across = shift(before, dy=1) if i % 2 == 0 else shift(after, dy=-1)
        mine, other = collide(
            table, pieces, [block, after, across, before], weights[:, i * cells : (i + 1) * cells]
        )
        got = shift(other, dz=1)
        results.append((mine + got.astype(jnp.float32)).reshape(-1, 1, *density.shape[2:]))
    return transported, jnp.concatenate(results, 1)


def solution(mesh):
    return jax.shard_map(
        local,
        mesh=mesh,
        in_specs=(
            P("vel", "space", None, None),
            P("space", None, None),
            P("vel"),
            P("vel"),
            P("space", None, "vel"),
        ),
        out_specs=(P("vel", "space", None, None), P("vel", "space", None, None)),
        check_vma=False,
    )
```

```python
import jax
import jax.numpy as jnp
from jax import lax
from jax.experimental import pallas as pl
from jax.experimental.pallas import tpu as pltpu
from jax.sharding import PartitionSpec as P

SLICES = 16
CHUNKS = ((0,), (1,), (2,), (3,))
BOTH = ("vel", "space")
FLAT = [
    (y, z, x, h, c)
    for y in range(4)
    for z in range(2)
    for x in range(4)
    for h in range(2)
    for c in range(2)
]
BF16, F32 = jnp.bfloat16, jnp.float32
ANY = pl.BlockSpec(memory_space=pl.ANY)
VMEM = pl.BlockSpec(memory_space=pltpu.VMEM)
SMEM = pl.BlockSpec(memory_space=pltpu.SMEM)


def rank(y, z, x, h, c):
    return ((y % 4) * 2 + z) * 16 + (x % 4) * 4 + h * 2 + c


def shift(value, dy=0, dz=0, dx=0, dh=0, dc=0):
    pairs = [
        (rank(y, z, x, h, c), rank(y + dy, z ^ dz, x + dx, h ^ dh, c ^ dc)) for y, z, x, h, c in FLAT
    ]
    return lax.ppermute(value, BOTH, pairs)


def after(value, *earlier):
    return lax.optimization_barrier((value, earlier))[0]


def shape(dims, dtype):
    return jax.ShapeDtypeStruct(dims, dtype)


def pack(density, limiter):
    rows = density.shape[0]

    def kernel(d_ref, l_ref, up_ref, down_ref):
        up_ref[:rows] = d_ref[:, 2:].astype(BF16)
        down_ref[:rows] = d_ref[:, :2].astype(BF16)
        codes = l_ref[...].astype(F32).astype(BF16)
        up_ref[rows] = codes[2:]
        down_ref[rows] = codes[:2]

    out = shape((rows + 1, 2, *density.shape[2:]), BF16)
    return pl.pallas_call(
        kernel, out_shape=(out, out), in_specs=[VMEM, VMEM], out_specs=(VMEM, VMEM), name="pack"
    )(density, limiter)


def split_slice(kernel_slice):
    def kernel(k_ref, keep_ref, send_ref):
        z = lax.axis_index("vel") & 1
        for y in range(4):
            cols = pl.ds(y * 128, 128)
            keep_ref[:, cols] = k_ref[y, z].astype(F32).T.astype(BF16)
            send_ref[:, cols] = k_ref[y, 1 - z].astype(F32).T.astype(BF16)

    out = shape((128, 512), BF16)
    return pl.pallas_call(
        kernel, out_shape=(out, out), in_specs=[VMEM], out_specs=(VMEM, VMEM), name="split_slice"
    )(kernel_slice.reshape(4, 2, 128, 128))


def transport(density, limiter, heading, courant, below, above):
    rows = density.shape[0]
    step = 32

    def kernel(h_ref, c_ref, d_ref, lo_ref, hi_ref, lo_code, hi_code, l_ref, t_ref, w_ref, *m_refs):
        first = pl.program_id(0) * step
        codes = [lo_code[0, 1].astype(F32)] + [l_ref[i].astype(F32) for i in range(4)]
        codes.append(hi_code[0, 0].astype(F32))
        minmod = [code == 1 for code in codes]
        central = [code == 2 for code in codes]

        def one(j, _):
            cell = [lo_ref[j, 0].astype(F32), lo_ref[j, 1].astype(F32)]
            cell += [d_ref[pl.ds(pl.multiple_of(j * 32 + 8 * i, 8), 8), :] for i in range(4)]
            cell += [hi_ref[j, 0].astype(F32), hi_ref[j, 1].astype(F32)]
            ahead = h_ref[first + j]
            half = 0.5 * (2 * ahead - 1).astype(F32)
            number = c_ref[first + j]
            diff = [cell[i + 1] - cell[i] for i in range(7)]
            rebuilt = []
            for i in range(6):
                left, right = diff[i], diff[i + 1]
                small = jnp.where(left > 0, jnp.minimum(left, right), jnp.maximum(left, right))
                small = jnp.where(left * right > 0, small, 0.0)
                slope = jnp.where(
                    minmod[i], small, jnp.where(central[i], 0.5 * (left + right), 0.0)
                )
                rebuilt.append(cell[i + 1] + half * slope)
            forward = jnp.full((8, 128), ahead, jnp.int32) == 1
            for i in range(4):
                upstream = jnp.where(forward, rebuilt[i], rebuilt[i + 2])
                value = cell[i + 2] - number * (rebuilt[i + 1] - upstream)
                t_ref[pl.ds(pl.multiple_of(j * 32 + 8 * i, 8), 8), :] = value
            return 0

        lax.fori_loop(0, step, one, 0, unroll=4)
        for m_ref, layers in zip(m_refs, CHUNKS, strict=True):
            for place, i in enumerate(layers):
                for y in range(8):
                    cols = pl.ds(place * 1024 + y * 128, 128)
                    m_ref[:, cols] = t_ref[pl.ds(8 * i + y, step, stride=32), :].astype(BF16)

        @pl.when(pl.program_id(0) % 2 == 0)
        def _():
            for i in range(4):
                w_ref[0, i] = t_ref[8 * i : 8 * i + 8, :].astype(BF16)

    halo = pl.BlockSpec((step, 2, 8, 128), lambda i: (i, 0, 0, 0))
    code = pl.BlockSpec((1, 2, 8, 128), lambda i: (rows, 0, 0, 0))
    flat = pl.BlockSpec((step * 32, 128), lambda i: (i, 0))
    outs = pl.pallas_call(
        kernel,
        grid=(rows // step,),
        out_shape=(shape((rows * 32, 128), F32), shape((2, 4, 8, 128), BF16))
        + tuple(shape((rows, 1024 * len(layers)), BF16) for layers in CHUNKS),
        in_specs=[
            SMEM,
            SMEM,
            flat,
            halo,
            halo,
            code,
            code,
            pl.BlockSpec((4, 8, 128), lambda i: (0, 0, 0)),
        ],
        out_specs=(flat, pl.BlockSpec((1, 4, 8, 128), lambda i: (i // 2, 0, 0, 0)))
        + tuple(pl.BlockSpec((step, 1024 * len(layers)), lambda i: (i, 0)) for layers in CHUNKS),
        cost_estimate=pl.CostEstimate(flops=2 << 20, bytes_accessed=6 << 20, transcendentals=0),
        name="transport",
    )(heading, courant, density.reshape(rows * 32, 128), below, above, below, above, limiter)
    return outs[0].reshape(density.shape), outs[1], outs[2:]


ORDER = [(0, 0), (0, 1), (3, 0), (3, 1), (1, 0), (1, 1), (2, 0), (2, 1)]


def weight_rows():
    vel, space = lax.axis_index("vel"), lax.axis_index("space")
    y, z = vel >> 1, vel & 1
    x, h, c = space >> 2, (space >> 1) & 1, space & 1
    rows = []
    for dc in range(2):
        for dx, dh in ORDER:
            v = (((x + dx) & 3) << 1) + (h ^ dh)
            rows.append(((((v >> 1) - y) & 3) << 2) + (((v & 1) ^ z) << 1) + (c ^ dc))
    return y, rows


def collide(layers, pieces, blocks, weights):
    cells = blocks[0].shape[1]
    tile = 512

    def kernel(*refs):
        w_parts = refs[:4]
        slabs = refs[4:14]
        parts = refs[14:18]
        mine_ref, other_ref, k_ref, m_ref, w_ref, sem_k, sem_m = refs[18:]
        y, places = weight_rows()
        loads = []
        for d in range(4):
            at = pl.multiple_of(((y + d) & 3) * 128, 128)
            loads.append(pltpu.make_async_copy(parts[d], m_ref.at[pl.ds(at, 128)], sem_m.at[d]))
        row, starts = 0, []
        for i in range(10):
            n = slabs[i].shape[0]
            loads.append(pltpu.make_async_copy(slabs[i], k_ref.at[pl.ds(row, n)], sem_k.at[i]))
            starts.append(row // 256)
            row += n
        for load in loads:
            load.start()
        for d in range(4):
            for i, layer in enumerate(layers):
                w_ref[4 * d : 4 * d + 4, i] = w_parts[d][:, layer].astype(F32)
        for load in loads[:4]:
            load.wait()
        for t in range(cells // tile):
            cols = pl.ds(t * tile, tile)
            moved = m_ref[:, cols]
            total = jnp.zeros((256, tile), F32)
            for s in range(SLICES):
                if t == 0 and s in starts:
                    loads[4 + starts.index(s)].wait()
                product = jnp.dot(
                    k_ref[s * 256 : (s + 1) * 256], moved, preferred_element_type=F32
                )
                lines = [
                    w_ref[places[s], t // 2, pl.ds((t % 2) * 4 + i, 1), :] for i in range(tile // 128)
                ]
                total = total + jnp.concatenate(lines, 1) * product
            mine_ref[:, cols] = total[:128]
            other_ref[:, cols] = total[128:].astype(BF16)

    return pl.pallas_call(
        kernel,
        out_shape=(shape((128, cells), F32), shape((128, cells), BF16)),
        in_specs=[VMEM] * 4 + [ANY] * 14,
        out_specs=(VMEM, VMEM),
        scratch_shapes=[
            pltpu.VMEM((SLICES * 256, 512), BF16),
            pltpu.VMEM((512, cells), BF16),
            pltpu.VMEM((SLICES, len(layers), 8, 128), F32),
            pltpu.SemaphoreType.DMA((10,)),
            pltpu.SemaphoreType.DMA((4,)),
        ],
        compiler_params=pltpu.CompilerParams(vmem_limit_bytes=24 << 20),
        cost_estimate=pl.CostEstimate(
            flops=2 * SLICES * 256 * 512 * cells, bytes_accessed=6 << 20, transcendentals=0
        ),
        name="collide",
    )(*weights, *pieces, *blocks)


def combine(mine, got):
    step = 32
    n = len(CHUNKS)

    def kernel(*refs):
        o_ref = refs[-1]
        for a_ref, b_ref, layers in zip(refs[:n], refs[n : 2 * n], CHUNKS, strict=True):
            for place, i in enumerate(layers):
                for y in range(8):
                    cols = pl.ds(place * 1024 + y * 128, 128)
                    o_ref[pl.ds(8 * i + y, step, stride=32), :] = a_ref[:, cols] + b_ref[
                        :, cols
                    ].astype(F32)

    blocks = [pl.BlockSpec((step, 1024 * len(layers)), lambda i: (i, 0)) for layers in CHUNKS]
    return pl.pallas_call(
        kernel,
        grid=(128 // step,),
        out_shape=shape((128 * 32, 128), F32),
        in_specs=blocks + blocks,
        out_specs=pl.BlockSpec((step * 32, 128), lambda i: (i, 0)),
        cost_estimate=pl.CostEstimate(flops=1 << 19, bytes_accessed=5 << 20, transcendentals=0),
        name="combine",
    )(*mine, *got)


def local(density, limiter, heading, courant, kernel_slices):
    size = lax.axis_size("space")
    up = [(i, i + 1) for i in range(size - 1)]

    upper, lower = pack(density, limiter)
    below = lax.ppermute(upper, "space", up)
    above = lax.ppermute(lower, "space", [(j, i) for i, j in up])

    keep, send = split_slice(after(kernel_slices[0], upper))
    here = shift(send, dz=1)
    far = shift(keep, dh=1)
    cross = shift(send, dz=1, dh=1)
    base = jnp.concatenate([keep, here, far, cross], 0)
    one = shift(base, dx=1)
    three = shift(base, dx=-1)

    below, above = after((below, above), base)
    transported, own, chunks = transport(density, limiter, heading, courant, below, above)

    gathered, done = [], None
    for i, block in enumerate(chunks):
        if done is not None:
            block = after(block, *done)
        done = before, behind = shift(block, dy=1), shift(block, dy=-1)
        across = shift(before, dy=1) if i % 2 else shift(behind, dy=-1)
        gathered.append([block, behind, across, before])

    own = after(own, one, three)
    rows = jnp.concatenate([own, shift(own, dz=1)], 0)
    weights = [rows, shift(rows, dy=-1), shift(rows, dy=2), shift(rows, dy=1)]

    pieces = [base, one, three, shift(one[:256], dx=1), shift(three[256:], dx=-1)]
    pieces = pieces + [shift(p, dc=1) for p in pieces]

    mine, got = [], []
    for layers, blocks in zip(CHUNKS, gathered, strict=True):
        m, other = collide(layers, pieces, blocks, weights)
        mine.append(m)
        got.append(shift(other, dz=1))
    return transported, combine(mine, got).reshape(density.shape)


def solution(mesh):
    return jax.shard_map(
        local,
        mesh=mesh,
        in_specs=(
            P("vel", "space", None, None),
            P("space", None, None),
            P("vel"),
            P("vel"),
            P("space", None, "vel"),
        ),
        out_specs=(P("vel", "space", None, None), P("vel", "space", None, None)),
        check_vma=False,
    )
```

```python
import jax
import jax.numpy as jnp
from jax import lax
from jax.experimental import pallas as pl
from jax.experimental.pallas import tpu as pltpu
from jax.sharding import PartitionSpec as P

SLICES = 16
BLOCKS = ((1, 2), (0, 3))
BOTH = ("vel", "space")
FLAT = [
    (y, z, x, h, c)
    for y in range(4)
    for z in range(2)
    for x in range(4)
    for h in range(2)
    for c in range(2)
]
BF16, F32 = jnp.bfloat16, jnp.float32
ANY = pl.BlockSpec(memory_space=pl.ANY)
VMEM = pl.BlockSpec(memory_space=pltpu.VMEM)
SMEM = pl.BlockSpec(memory_space=pltpu.SMEM)


def rank(y, z, x, h, c):
    return ((y % 4) * 2 + z) * 16 + (x % 4) * 4 + h * 2 + c


def shift(value, dy=0, dz=0, dx=0, dh=0, dc=0):
    pairs = [
        (rank(y, z, x, h, c), rank(y + dy, z ^ dz, x + dx, h ^ dh, c ^ dc)) for y, z, x, h, c in FLAT
    ]
    return lax.ppermute(value, BOTH, pairs)


def after(value, *earlier):
    return lax.optimization_barrier((value, earlier))[0]


def shape(dims, dtype):
    return jax.ShapeDtypeStruct(dims, dtype)


def pack(density, limiter):
    rows = density.shape[0]

    def kernel(d_ref, l_ref, first_ref, second_ref, inner_ref):
        core = lax.axis_index("space") & 1

        def fill(outer, following, pair):
            first_ref[:rows] = d_ref[:, outer].astype(BF16)
            first_ref[rows] = l_ref[outer].astype(F32).astype(BF16)
            for i in range(2):
                first_ref[rows + 1 + i] = d_ref[64 * i, following].astype(BF16)
            second_ref[...] = d_ref[:, following].astype(BF16)
            inner_ref[:rows] = d_ref[:, pair : pair + 2].astype(BF16)
            inner_ref[rows] = l_ref[pair : pair + 2].astype(F32).astype(BF16)

        @pl.when(core == 1)
        def _():
            fill(3, 2, 0)

        @pl.when(core == 0)
        def _():
            fill(0, 1, 2)

    dims = density.shape[2:]
    return pl.pallas_call(
        kernel,
        out_shape=(
            shape((rows + 3, *dims), BF16),
            shape((rows, *dims), BF16),
            shape((rows + 1, 2, *dims), BF16),
        ),
        in_specs=[VMEM, VMEM],
        out_specs=(VMEM, VMEM, VMEM),
        name="pack",
    )(density, limiter)


def split_slice(kernel_slice):
    def kernel(k_ref, o_ref):
        z = lax.axis_index("vel") & 1
        for y in range(4):
            cols = pl.ds(y * 128, 128)
            o_ref[:128, cols] = k_ref[y, 1 - z].astype(F32).T.astype(BF16)
            o_ref[128:, cols] = k_ref[y, z].astype(F32).T.astype(BF16)

    return pl.pallas_call(
        kernel, out_shape=shape((256, 512), BF16), in_specs=[VMEM], out_specs=VMEM, name="split_slice"
    )(kernel_slice.reshape(4, 2, 128, 128))


def update(cells, codes, ahead, number, layers):
    half = 0.5 * (2 * ahead - 1).astype(F32)
    forward = jnp.full((8, 128), ahead, jnp.int32) == 1
    rebuilt = {}
    for i in sorted({i + d for i in layers for d in (-1, 0, 1)}):
        left, right = cells[i] - cells[i - 1], cells[i + 1] - cells[i]
        small = jnp.where(left > 0, jnp.minimum(left, right), jnp.maximum(left, right))
        small = jnp.where(left * right > 0, small, 0.0)
        slope = jnp.where(
            codes[i] == 1, small, jnp.where(codes[i] == 2, 0.5 * (left + right), 0.0)
        )
        rebuilt[i] = cells[i] + half * slope
    return [
        cells[i] - number * (rebuilt[i] - jnp.where(forward, rebuilt[i - 1], rebuilt[i + 1]))
        for i in layers
    ]


STEP = 32


def transport_specs(rows):
    return [
        SMEM,
        SMEM,
        pl.BlockSpec((STEP, 4, 8, 128), lambda i: (i, 0, 0, 0)),
        pl.BlockSpec((4, 8, 128), lambda i: (0, 0, 0)),
        pl.BlockSpec((STEP, 8, 128), lambda i: (i, 0, 0)),
        pl.BlockSpec((1, 8, 128), lambda i: (rows, 0, 0)),
        pl.BlockSpec((STEP, 2, 8, 128), lambda i: (i, 0, 0, 0)),
        pl.BlockSpec((1, 2, 8, 128), lambda i: (rows, 0, 0, 0)),
    ]


def outer_codes(core, l_ref, first_code, inner_code):
    codes = {i: l_ref[i].astype(F32) for i in range(4)}
    codes[-1] = jnp.where(core == 0, first_code[0].astype(F32), inner_code[0, 1].astype(F32))
    codes[4] = jnp.where(core == 0, inner_code[0, 0].astype(F32), first_code[0].astype(F32))
    return codes


def neighbours(core, j, first_ref, inner_ref, second=None):
    a, b = inner_ref[j, 0].astype(F32), inner_ref[j, 1].astype(F32)
    first = first_ref[j].astype(F32)
    cells = {-1: jnp.where(core == 0, first, b), 4: jnp.where(core == 0, a, first)}
    if second is not None:
        second = second.astype(F32)
        cells[-2] = jnp.where(core == 0, second, a)
        cells[5] = jnp.where(core == 0, b, second)
    return cells


def flatten(m_ref, t_ref, places):
    for place, i in enumerate(places):
        turned = jnp.swapaxes(t_ref[:, i], 0, 1)
        for y in range(8):
            m_ref[:, pl.ds(place * 1024 + y * 128, 128)] = turned[y].astype(BF16)


def transport_inner(density, limiter, heading, courant, first, inner):
    rows = density.shape[0]

    def kernel(
        h_ref, c_ref, d_ref, l_ref, first_ref, first_code, inner_ref, inner_code, next_ref, m_ref, w_ref, t_ref
    ):
        core = lax.axis_index("space") & 1
        start = pl.program_id(0) * STEP
        codes = outer_codes(core, l_ref, first_code, inner_code)

        def one(j, _):
            cells = {i: d_ref[j, i] for i in range(4)}
            cells.update(neighbours(core, j, first_ref, inner_ref))
            values = update(cells, codes, h_ref[start + j], c_ref[start + j], (1, 2))
            for i, value in enumerate(values):
                t_ref[j, i] = value
            return 0

        lax.fori_loop(0, STEP, one, 0, unroll=4)
        flatten(m_ref, t_ref, (0, 1))

        @pl.when(pl.program_id(0) % 2 == 0)
        def _():
            cells = {i: d_ref[0, i] for i in range(4)}
            cells.update(neighbours(core, 0, first_ref, inner_ref, next_ref[0]))
            values = update(cells, codes, h_ref[start], c_ref[start], range(4))
            for i, value in enumerate(values):
                w_ref[0, i] = value.astype(BF16)

    return pl.pallas_call(
        kernel,
        grid=(rows // STEP,),
        out_shape=(shape((rows, 2048), BF16), shape((2, 4, 8, 128), BF16)),
        in_specs=transport_specs(rows)
        + [pl.BlockSpec((1, 8, 128), lambda i: (rows + 1 + i // 2, 0, 0))],
        out_specs=(
            pl.BlockSpec((STEP, 2048), lambda i: (i, 0)),
            pl.BlockSpec((1, 4, 8, 128), lambda i: (i // 2, 0, 0, 0)),
        ),
        scratch_shapes=[pltpu.VMEM((STEP, 2, 8, 128), F32)],
        cost_estimate=pl.CostEstimate(flops=2 << 20, bytes_accessed=3 << 20, transcendentals=0),
        name="transport_inner",
    )(heading, courant, density, limiter, first, first, inner, inner, first)


def transport(density, limiter, heading, courant, first, second, inner):
    rows = density.shape[0]

    def kernel(
        h_ref, c_ref, d_ref, l_ref, first_ref, first_code, inner_ref, inner_code, next_ref, t_ref, m_ref
    ):
        core = lax.axis_index("space") & 1
        start = pl.program_id(0) * STEP
        codes = outer_codes(core, l_ref, first_code, inner_code)

        def one(j, _):
            cells = {i: d_ref[j, i] for i in range(4)}
            cells.update(neighbours(core, j, first_ref, inner_ref, next_ref[j]))
            values = update(cells, codes, h_ref[start + j], c_ref[start + j], range(4))
            for i, value in enumerate(values):
                t_ref[j, i] = value
            return 0

        lax.fori_loop(0, STEP, one, 0, unroll=4)
        flatten(m_ref, t_ref, (0, 3))

    return pl.pallas_call(
        kernel,
        grid=(rows // STEP,),
        out_shape=(shape(density.shape, F32), shape((rows, 2048), BF16)),
        in_specs=transport_specs(rows) + [pl.BlockSpec((STEP, 8, 128), lambda i: (i, 0, 0))],
        out_specs=(
            pl.BlockSpec((STEP, 4, 8, 128), lambda i: (i, 0, 0, 0)),
            pl.BlockSpec((STEP, 2048), lambda i: (i, 0)),
        ),
        cost_estimate=pl.CostEstimate(flops=4 << 20, bytes_accessed=6 << 20, transcendentals=0),
        name="transport",
    )(heading, courant, density, limiter, first, first, inner, inner, second)


ORDER = [(0, 0), (0, 1), (3, 0), (3, 1), (1, 0), (1, 1), (2, 0), (2, 1)]


def weight_rows():
    vel, space = lax.axis_index("vel"), lax.axis_index("space")
    y, z = vel >> 1, vel & 1
    x, h, c = space >> 2, (space >> 1) & 1, space & 1
    rows = []
    for dc in range(2):
        for dx, dh in ORDER:
            v = (((x + dx) & 3) << 1) + (h ^ dh)
            rows.append(((((v >> 1) - y) & 3) << 2) + (((v & 1) ^ z) << 1) + (c ^ dc))
    return y, rows


def collide(layer, place, pieces, blocks, weights):
    cells = 1024
    tile = 512
    columns = pl.ds(place * cells, cells)
    targets = [(0, 0, 128), (1, 0, 128), (3, 0, 128), (2, 0, 64), (2, 64, 64)]

    def kernel(*refs):
        w_parts = refs[:4]
        slabs = refs[4:14]
        parts = refs[14:19]
        mine_ref, other_ref, k_ref, m_ref, w_ref, sem_k, sem_m = refs[19:]
        y, places = weight_rows()
        loads = []
        for i, (d, skip, n) in enumerate(targets):
            at = pl.multiple_of(((y + d) & 3) * 128 + skip, 64)
            loads.append(
                pltpu.make_async_copy(
                    parts[i].at[:, columns], m_ref.at[pl.ds(at, n)], sem_m.at[i]
                )
            )
        row, starts = 0, []
        for i in range(10):
            n = slabs[i].shape[0]
            loads.append(pltpu.make_async_copy(slabs[i], k_ref.at[pl.ds(row, n)], sem_k.at[i]))
            starts.append(row // 256)
            row += n
        for load in loads:
            load.start()
        for d in range(4):
            w_ref[4 * d : 4 * d + 4] = w_parts[d][:, layer].astype(F32)
        for load in loads[:5]:
            load.wait()
        for t in range(cells // tile):
            cols = pl.ds(t * tile, tile)
            moved = m_ref[:, cols]
            total = jnp.zeros((256, tile), F32)
            for s in range(SLICES):
                if t == 0 and s in starts:
                    loads[5 + starts.index(s)].wait()
                product = jnp.dot(
                    k_ref[s * 256 : (s + 1) * 256], moved, preferred_element_type=F32
                )
                lines = [w_ref[places[s], pl.ds(t * 4 + i, 1), :] for i in range(tile // 128)]
                total = total + jnp.concatenate(lines, 1) * product
            mine_ref[:, cols] = total[:128]
            other_ref[:, cols] = total[128:].astype(BF16)

    return pl.pallas_call(
        kernel,
        out_shape=(shape((128, cells), F32), shape((128, cells), BF16)),
        in_specs=[VMEM] * 4 + [ANY] * 15,
        out_specs=(VMEM, VMEM),
        scratch_shapes=[
            pltpu.VMEM((SLICES * 256, 512), BF16),
            pltpu.VMEM((512, cells), BF16),
            pltpu.VMEM((SLICES, 8, 128), F32),
            pltpu.SemaphoreType.DMA((10,)),
            pltpu.SemaphoreType.DMA((5,)),
        ],
        compiler_params=pltpu.CompilerParams(vmem_limit_bytes=24 << 20),
        cost_estimate=pl.CostEstimate(
            flops=2 * SLICES * 256 * 512 * cells, bytes_accessed=6 << 20, transcendentals=0
        ),
        name="collide",
    )(*weights, *pieces, *blocks)


def combine(layer, mine, got, result):
    step = 64

    def kernel(a_ref, b_ref, *refs):
        o_ref = refs[-1]
        total = a_ref[...] + b_ref[...].astype(F32)
        lines = jnp.stack([total[:, y * 128 : (y + 1) * 128] for y in range(8)], 0)
        o_ref[:, 0] = jnp.swapaxes(lines, 0, 1)

    block = pl.BlockSpec((step, 1024), lambda i: (i, 0))
    given = [] if result is None else [result]
    return pl.pallas_call(
        kernel,
        grid=(128 // step,),
        out_shape=shape((128, 4, 8, 128), F32),
        in_specs=[block, block] + [ANY] * len(given),
        out_specs=pl.BlockSpec((step, 1, 8, 128), lambda i: (i, layer, 0, 0)),
        input_output_aliases={2: 0} if given else {},
        cost_estimate=pl.CostEstimate(flops=1 << 17, bytes_accessed=5 << 18, transcendentals=0),
        name="combine",
    )(mine, got, *given)


def local(density, limiter, heading, courant, kernel_slices):
    size = lax.axis_size("space")
    beside = [(i, i + 1) for i in range(1, size - 1, 2)]
    beside = beside + [(j, i) for i, j in beside]

    own_slice = split_slice(kernel_slices[0])
    partner = shift(own_slice, dz=1)
    first, second, inner = pack(after(density, own_slice), limiter)
    first = lax.ppermute(first, "space", beside)
    inner = shift(inner, dc=1)

    crossing = jnp.concatenate([partner[128:], own_slice[:128]], 0)
    cross = shift(crossing, dz=1, dh=1)
    first = after(first, crossing)
    second = lax.ppermute(after(second, first), "space", beside)
    block, own = transport_inner(density, limiter, heading, courant, first, inner)

    base = jnp.concatenate([own_slice[128:], partner[:128], after(cross, block)], 0)
    one = shift(base, dx=1)
    three = shift(base, dx=-1)
    pieces = [base, one, three, shift(one[:256], dx=1), shift(three[256:], dx=-1)]
    swapped = [shift(p, dc=1) for p in pieces]
    pieces = pieces + swapped

    def gather(block, *earlier):
        before, behind = after((shift(block, dy=1), shift(block, dy=-1)), *earlier)
        return [block, behind, before, shift(before[:64], dy=1), shift(behind[64:], dy=-1)]

    inside = gather(after(block, swapped[0]), second)
    rows = jnp.concatenate([own, shift(own, dz=1)], 0)
    second = after(second, inside[1], inside[2])
    transported, block = transport(density, limiter, heading, courant, first, second, inner)
    rows = after(rows, block, swapped[1], swapped[2])
    block = after(block, inside[3], inside[4])
    weights = [rows, shift(rows, dy=-1), shift(rows, dy=2), shift(rows, dy=1)]
    outside = gather(block)

    result, got = None, []
    for layers, blocks in zip(BLOCKS, (inside, outside), strict=True):
        for place, layer in enumerate(layers):
            mine, other = collide(layer, place, pieces, blocks, weights)
            weights = after(weights, mine, *got[-1:])
            got.append(shift(other, dz=1))
            result = combine(layer, mine, got[-1], result)
    return transported, result


def solution(mesh):
    return jax.shard_map(
        local,
        mesh=mesh,
        in_specs=(
            P("vel", "space", None, None),
            P("space", None, None),
            P("vel"),
            P("vel"),
            P("space", None, "vel"),
        ),
        out_specs=(P("vel", "space", None, None), P("vel", "space", None, None)),
        check_vma=False,
    )
```

```python
import jax
import jax.numpy as jnp
from jax import lax
from jax.experimental import pallas as pl
from jax.experimental.pallas import tpu as pltpu
from jax.sharding import PartitionSpec as P

SLICES = 16
BLOCKS = ((1, 2), (0, 3))
BOTH = ("vel", "space")
FLAT = [
    (y, z, x, h, c)
    for y in range(4)
    for z in range(2)
    for x in range(4)
    for h in range(2)
    for c in range(2)
]
BF16, F32 = jnp.bfloat16, jnp.float32
ANY = pl.BlockSpec(memory_space=pl.ANY)
VMEM = pl.BlockSpec(memory_space=pltpu.VMEM)
SMEM = pl.BlockSpec(memory_space=pltpu.SMEM)


def rank(y, z, x, h, c):
    return ((y % 4) * 2 + z) * 16 + (x % 4) * 4 + h * 2 + c


def shift(value, dy=0, dz=0, dx=0, dh=0, dc=0):
    pairs = [
        (rank(y, z, x, h, c), rank(y + dy, z ^ dz, x + dx, h ^ dh, c ^ dc)) for y, z, x, h, c in FLAT
    ]
    return lax.ppermute(value, BOTH, pairs)


def after(value, *earlier):
    return lax.optimization_barrier((value, earlier))[0]


def shape(dims, dtype):
    return jax.ShapeDtypeStruct(dims, dtype)


def pack(density, limiter):
    rows = density.shape[0]

    def kernel(d_ref, l_ref, first_ref, second_ref, inner_ref):
        core = lax.axis_index("space") & 1

        def fill(outer, following, pair):
            first_ref[:rows] = d_ref[:, outer].astype(BF16)
            first_ref[rows] = l_ref[outer].astype(F32).astype(BF16)
            for i in range(2):
                first_ref[rows + 1 + i] = d_ref[64 * i, following].astype(BF16)
            second_ref[...] = d_ref[:, following].astype(BF16)
            inner_ref[:rows] = d_ref[:, pair : pair + 2].astype(BF16)
            inner_ref[rows] = l_ref[pair : pair + 2].astype(F32).astype(BF16)

        @pl.when(core == 1)
        def _():
            fill(3, 2, 0)

        @pl.when(core == 0)
        def _():
            fill(0, 1, 2)

    dims = density.shape[2:]
    return pl.pallas_call(
        kernel,
        out_shape=(
            shape((rows + 3, *dims), BF16),
            shape((rows, *dims), BF16),
            shape((rows + 1, 2, *dims), BF16),
        ),
        in_specs=[VMEM, VMEM],
        out_specs=(VMEM, VMEM, VMEM),
        name="pack",
    )(density, limiter)


def split_slice(kernel_slice):
    def kernel(k_ref, o_ref):
        z = lax.axis_index("vel") & 1
        for y in range(4):
            cols = pl.ds(y * 128, 128)
            o_ref[:128, cols] = k_ref[y, 1 - z].astype(F32).T.astype(BF16)
            o_ref[128:, cols] = k_ref[y, z].astype(F32).T.astype(BF16)

    return pl.pallas_call(
        kernel, out_shape=shape((256, 512), BF16), in_specs=[VMEM], out_specs=VMEM, name="split_slice"
    )(kernel_slice.reshape(4, 2, 128, 128))


def update(cells, codes, ahead, number, layers):
    half = 0.5 * (2 * ahead - 1).astype(F32)
    forward = jnp.full((8, 128), ahead, jnp.int32) == 1
    rebuilt = {}
    for i in sorted({i + d for i in layers for d in (-1, 0, 1)}):
        left, right = cells[i] - cells[i - 1], cells[i + 1] - cells[i]
        small = jnp.where(left > 0, jnp.minimum(left, right), jnp.maximum(left, right))
        small = jnp.where(left * right > 0, small, 0.0)
        slope = jnp.where(
            codes[i] == 1, small, jnp.where(codes[i] == 2, 0.5 * (left + right), 0.0)
        )
        rebuilt[i] = cells[i] + half * slope
    return [
        cells[i] - number * (rebuilt[i] - jnp.where(forward, rebuilt[i - 1], rebuilt[i + 1]))
        for i in layers
    ]


STEP = 32


def transport_specs(rows):
    return [
        SMEM,
        SMEM,
        pl.BlockSpec((STEP, 4, 8, 128), lambda i: (i, 0, 0, 0)),
        pl.BlockSpec((4, 8, 128), lambda i: (0, 0, 0)),
        pl.BlockSpec((STEP, 8, 128), lambda i: (i, 0, 0)),
        pl.BlockSpec((1, 8, 128), lambda i: (rows, 0, 0)),
        pl.BlockSpec((STEP, 2, 8, 128), lambda i: (i, 0, 0, 0)),
        pl.BlockSpec((1, 2, 8, 128), lambda i: (rows, 0, 0, 0)),
    ]


def outer_codes(core, l_ref, first_code, inner_code):
    codes = {i: l_ref[i].astype(F32) for i in range(4)}
    codes[-1] = jnp.where(core == 0, first_code[0].astype(F32), inner_code[0, 1].astype(F32))
    codes[4] = jnp.where(core == 0, inner_code[0, 0].astype(F32), first_code[0].astype(F32))
    return codes


def neighbours(core, j, first_ref, inner_ref, second=None):
    a, b = inner_ref[j, 0].astype(F32), inner_ref[j, 1].astype(F32)
    first = first_ref[j].astype(F32)
    cells = {-1: jnp.where(core == 0, first, b), 4: jnp.where(core == 0, a, first)}
    if second is not None:
        second = second.astype(F32)
        cells[-2] = jnp.where(core == 0, second, a)
        cells[5] = jnp.where(core == 0, b, second)
    return cells


def flatten(m_ref, t_ref, places):
    for place, i in enumerate(places):
        turned = jnp.swapaxes(t_ref[:, i], 0, 1)
        for y in range(8):
            m_ref[:, pl.ds(place * 1024 + y * 128, 128)] = turned[y].astype(BF16)


def transport_inner(density, limiter, heading, courant, first, inner):
    rows = density.shape[0]

    def kernel(
        h_ref, c_ref, d_ref, l_ref, first_ref, first_code, inner_ref, inner_code, next_ref, m_ref, w_ref, t_ref
    ):
        core = lax.axis_index("space") & 1
        start = pl.program_id(0) * STEP
        codes = outer_codes(core, l_ref, first_code, inner_code)

        def one(j, _):
            cells = {i: d_ref[j, i] for i in range(4)}
            cells.update(neighbours(core, j, first_ref, inner_ref))
            values = update(cells, codes, h_ref[start + j], c_ref[start + j], (1, 2))
            for i, value in enumerate(values):
                t_ref[j, i] = value
            return 0

        lax.fori_loop(0, STEP, one, 0, unroll=4)
        flatten(m_ref, t_ref, (0, 1))

        @pl.when(pl.program_id(0) % 2 == 0)
        def _():
            cells = {i: d_ref[0, i] for i in range(4)}
            cells.update(neighbours(core, 0, first_ref, inner_ref, next_ref[0]))
            values = update(cells, codes, h_ref[start], c_ref[start], range(4))
            for i, value in enumerate(values):
                w_ref[0, i] = value.astype(BF16)

    return pl.pallas_call(
        kernel,
        grid=(rows // STEP,),
        out_shape=(shape((rows, 2048), BF16), shape((2, 4, 8, 128), BF16)),
        in_specs=transport_specs(rows)
        + [pl.BlockSpec((1, 8, 128), lambda i: (rows + 1 + i // 2, 0, 0))],
        out_specs=(
            pl.BlockSpec((STEP, 2048), lambda i: (i, 0)),
            pl.BlockSpec((1, 4, 8, 128), lambda i: (i // 2, 0, 0, 0)),
        ),
        scratch_shapes=[pltpu.VMEM((STEP, 2, 8, 128), F32)],
        cost_estimate=pl.CostEstimate(flops=2 << 20, bytes_accessed=3 << 20, transcendentals=0),
        name="transport_inner",
    )(heading, courant, density, limiter, first, first, inner, inner, first)


def transport(density, limiter, heading, courant, first, second, inner):
    rows = density.shape[0]

    def kernel(
        h_ref, c_ref, d_ref, l_ref, first_ref, first_code, inner_ref, inner_code, next_ref, t_ref, m_ref
    ):
        core = lax.axis_index("space") & 1
        start = pl.program_id(0) * STEP
        codes = outer_codes(core, l_ref, first_code, inner_code)

        def one(j, _):
            cells = {i: d_ref[j, i] for i in range(4)}
            cells.update(neighbours(core, j, first_ref, inner_ref, next_ref[j]))
            values = update(cells, codes, h_ref[start + j], c_ref[start + j], range(4))
            for i, value in enumerate(values):
                t_ref[j, i] = value
            return 0

        lax.fori_loop(0, STEP, one, 0, unroll=4)
        flatten(m_ref, t_ref, (0, 3))

    return pl.pallas_call(
        kernel,
        grid=(rows // STEP,),
        out_shape=(shape(density.shape, F32), shape((rows, 2048), BF16)),
        in_specs=transport_specs(rows) + [pl.BlockSpec((STEP, 8, 128), lambda i: (i, 0, 0))],
        out_specs=(
            pl.BlockSpec((STEP, 4, 8, 128), lambda i: (i, 0, 0, 0)),
            pl.BlockSpec((STEP, 2048), lambda i: (i, 0)),
        ),
        cost_estimate=pl.CostEstimate(flops=4 << 20, bytes_accessed=6 << 20, transcendentals=0),
        name="transport",
    )(heading, courant, density, limiter, first, first, inner, inner, second)


ORDER = [(0, 0), (0, 1), (3, 0), (3, 1), (1, 0), (1, 1), (2, 0), (2, 1)]


def weight_rows():
    vel, space = lax.axis_index("vel"), lax.axis_index("space")
    y, z = vel >> 1, vel & 1
    x, h, c = space >> 2, (space >> 1) & 1, space & 1
    rows = []
    for dc in range(2):
        for dx, dh in ORDER:
            v = (((x + dx) & 3) << 1) + (h ^ dh)
            rows.append(((((v >> 1) - y) & 3) << 2) + (((v & 1) ^ z) << 1) + (c ^ dc))
    return y, rows


def collide(layer, place, pieces, blocks, weights):
    cells = 1024
    tile = 512
    columns = pl.ds(place * cells, cells)
    targets = [(0, 0, 128), (1, 0, 128), (3, 0, 128), (2, 0, 64), (2, 64, 64)]

    def kernel(*refs):
        w_parts = refs[:4]
        slabs = refs[4:14]
        parts = refs[14:19]
        mine_ref, other_ref, k_ref, m_ref, w_ref, sem_k, sem_m = refs[19:]
        y, places = weight_rows()
        loads = []
        for i, (d, skip, n) in enumerate(targets):
            at = pl.multiple_of(((y + d) & 3) * 128 + skip, 64)
            loads.append(
                pltpu.make_async_copy(
                    parts[i].at[:, columns], m_ref.at[pl.ds(at, n)], sem_m.at[i]
                )
            )
        row, starts = 0, []
        for i in range(10):
            n = slabs[i].shape[0]
            loads.append(pltpu.make_async_copy(slabs[i], k_ref.at[pl.ds(row, n)], sem_k.at[i]))
            starts.append(row // 256)
            row += n
        for load in loads:
            load.start()
        for d in range(4):
            w_ref[4 * d : 4 * d + 4] = w_parts[d][:, layer].astype(F32)
        for load in loads[:5]:
            load.wait()
        for t in range(cells // tile):
            cols = pl.ds(t * tile, tile)
            moved = m_ref[:, cols]
            total = jnp.zeros((256, tile), F32)
            for s in range(SLICES):
                if t == 0 and s in starts:
                    loads[5 + starts.index(s)].wait()
                product = jnp.dot(
                    k_ref[s * 256 : (s + 1) * 256], moved, preferred_element_type=F32
                )
                lines = [w_ref[places[s], pl.ds(t * 4 + i, 1), :] for i in range(tile // 128)]
                total = total + jnp.concatenate(lines, 1) * product
            mine_ref[:, cols] = total[:128]
            other_ref[:, cols] = total[128:].astype(BF16)

    return pl.pallas_call(
        kernel,
        out_shape=(shape((128, cells), F32), shape((128, cells), BF16)),
        in_specs=[VMEM] * 4 + [ANY] * 15,
        out_specs=(VMEM, VMEM),
        scratch_shapes=[
            pltpu.VMEM((SLICES * 256, 512), BF16),
            pltpu.VMEM((512, cells), BF16),
            pltpu.VMEM((SLICES, 8, 128), F32),
            pltpu.SemaphoreType.DMA((10,)),
            pltpu.SemaphoreType.DMA((5,)),
        ],
        compiler_params=pltpu.CompilerParams(vmem_limit_bytes=56 << 20),
        cost_estimate=pl.CostEstimate(
            flops=2 * SLICES * 256 * 512 * cells, bytes_accessed=6 << 20, transcendentals=0
        ),
        name="collide",
    )(*weights, *pieces, *blocks)


def combine(layer, mine, got, result):
    step = 64

    def kernel(a_ref, b_ref, *refs):
        o_ref = refs[-1]
        total = a_ref[...] + b_ref[...].astype(F32)
        lines = jnp.stack([total[:, y * 128 : (y + 1) * 128] for y in range(8)], 0)
        o_ref[:, 0] = jnp.swapaxes(lines, 0, 1)

    block = pl.BlockSpec((step, 1024), lambda i: (i, 0))
    given = [] if result is None else [result]
    return pl.pallas_call(
        kernel,
        grid=(128 // step,),
        out_shape=shape((128, 4, 8, 128), F32),
        in_specs=[block, block] + [ANY] * len(given),
        out_specs=pl.BlockSpec((step, 1, 8, 128), lambda i: (i, layer, 0, 0)),
        input_output_aliases={2: 0} if given else {},
        cost_estimate=pl.CostEstimate(flops=1 << 17, bytes_accessed=5 << 18, transcendentals=0),
        name="combine",
    )(mine, got, *given)


def local(density, limiter, heading, courant, kernel_slices):
    size = lax.axis_size("space")
    beside = [(i, i + 1) for i in range(1, size - 1, 2)]
    beside = beside + [(j, i) for i, j in beside]

    own_slice = split_slice(kernel_slices[0])
    partner = shift(own_slice, dz=1)
    first, second, inner = pack(after(density, own_slice), limiter)
    first = lax.ppermute(first, "space", beside)
    inner = shift(inner, dc=1)

    crossing = jnp.concatenate([partner[128:], own_slice[:128]], 0)
    cross = shift(crossing, dz=1, dh=1)
    first = after(first, crossing)
    second = lax.ppermute(after(second, first), "space", beside)
    block, own = transport_inner(density, limiter, heading, courant, first, inner)

    base = jnp.concatenate([own_slice[128:], partner[:128], after(cross, block)], 0)
    swapped = [shift(base, dc=1)]
    block = after(block, swapped[0])
    before, behind = shift(block, dy=1), shift(block, dy=-1)
    one, three, before, behind = after(
        (shift(base, dx=1), shift(base, dx=-1), before, behind)
    )
    pieces = [base, one, three, shift(one[:256], dx=1), shift(three[256:], dx=-1)]
    pieces = pieces + swapped + [shift(p, dc=1) for p in pieces[1:]]
    inside = [block, behind, before, shift(before[:64], dy=1), shift(behind[64:], dy=-1)]

    rows = after(jnp.concatenate([own, shift(own, dz=1)], 0), before)
    weights = [rows, shift(rows, dy=-1), shift(rows, dy=2), shift(rows, dy=1)]
    second = after(second, before)
    transported, block = transport(density, limiter, heading, courant, first, second, inner)
    before, behind = shift(block, dy=1), shift(block, dy=-1)
    outside = [block, behind, before, shift(before[:64], dy=1), shift(behind[64:], dy=-1)]

    results, got = [None], []
    for layers, blocks in zip(BLOCKS, (inside, outside), strict=True):
        for place, layer in enumerate(layers):
            mine, other = collide(layer, place, pieces, blocks, weights)
            weights = after(weights, mine, *got[-1:], *results[1:][-1:])
            got.append(shift(other, dz=1))
            results.append(combine(layer, mine, got[-1], results[-1]))
    return transported, results[-1]


def solution(mesh):
    return jax.shard_map(
        local,
        mesh=mesh,
        in_specs=(
            P("vel", "space", None, None),
            P("space", None, None),
            P("vel"),
            P("vel"),
            P("space", None, "vel"),
        ),
        out_specs=(P("vel", "space", None, None), P("vel", "space", None, None)),
        check_vma=False,
    )
```

```python
import jax
import jax.numpy as jnp
from jax import lax
from jax.experimental import pallas as pl
from jax.experimental.pallas import tpu as pltpu
from jax.sharding import PartitionSpec as P

SLICES = 16
BLOCKS = ((0, 1), (2, 3))
BOTH = ("vel", "space")
FLAT = [
    (y, z, x, h, c)
    for y in range(4)
    for z in range(2)
    for x in range(4)
    for h in range(2)
    for c in range(2)
]
BF16, F32 = jnp.bfloat16, jnp.float32
ANY = pl.BlockSpec(memory_space=pl.ANY)
VMEM = pl.BlockSpec(memory_space=pltpu.VMEM)
SMEM = pl.BlockSpec(memory_space=pltpu.SMEM)


def rank(y, z, x, h, c):
    return ((y % 4) * 2 + z) * 16 + (x % 4) * 4 + h * 2 + c


def shift(value, dy=0, dz=0, dx=0, dh=0, dc=0):
    pairs = [
        (rank(y, z, x, h, c), rank(y + dy, z ^ dz, x + dx, h ^ dh, c ^ dc)) for y, z, x, h, c in FLAT
    ]
    return lax.ppermute(value, BOTH, pairs)


def after(value, *earlier):
    return lax.optimization_barrier((value, earlier))[0]


def shape(dims, dtype):
    return jax.ShapeDtypeStruct(dims, dtype)


def pack(density, limiter):
    rows = density.shape[0]

    def kernel(d_ref, l_ref, away_ref, inner_ref):
        core = lax.axis_index("space") & 1

        def fill(o_ref, start):
            o_ref[:rows] = d_ref[:, start : start + 2].astype(BF16)
            o_ref[rows] = l_ref[start : start + 2].astype(F32).astype(BF16)

        @pl.when(core == 1)
        def _():
            fill(away_ref, 2)
            fill(inner_ref, 0)

        @pl.when(core == 0)
        def _():
            fill(away_ref, 0)
            fill(inner_ref, 2)

    out = shape((rows + 1, 2, *density.shape[2:]), BF16)
    return pl.pallas_call(
        kernel, out_shape=(out, out), in_specs=[VMEM, VMEM], out_specs=(VMEM, VMEM), name="pack"
    )(density, limiter)


def split_slice(kernel_slice):
    def kernel(k_ref, o_ref):
        z = lax.axis_index("vel") & 1
        for y in range(4):
            cols = pl.ds(y * 128, 128)
            o_ref[:128, cols] = k_ref[y, 1 - z].astype(F32).T.astype(BF16)
            o_ref[128:, cols] = k_ref[y, z].astype(F32).T.astype(BF16)

    return pl.pallas_call(
        kernel, out_shape=shape((256, 512), BF16), in_specs=[VMEM], out_specs=VMEM, name="split_slice"
    )(kernel_slice.reshape(4, 2, 128, 128))


def update(cells, codes, ahead, number, layers):
    half = 0.5 * (2 * ahead - 1).astype(F32)
    forward = jnp.full((8, 128), ahead, jnp.int32) == 1
    rebuilt = {}
    for i in sorted({i + d for i in layers for d in (-1, 0, 1)}):
        left, right = cells[i] - cells[i - 1], cells[i + 1] - cells[i]
        small = jnp.where(left > 0, jnp.minimum(left, right), jnp.maximum(left, right))
        small = jnp.where(left * right > 0, small, 0.0)
        slope = jnp.where(
            codes[i] == 1, small, jnp.where(codes[i] == 2, 0.5 * (left + right), 0.0)
        )
        rebuilt[i] = cells[i] + half * slope
    return [
        cells[i] - number * (rebuilt[i] - jnp.where(forward, rebuilt[i - 1], rebuilt[i + 1]))
        for i in layers
    ]


STEP = 32


def transport(density, limiter, heading, courant, away, inner):
    rows = density.shape[0]

    def kernel(
        h_ref, c_ref, d_ref, l_ref, away_ref, away_code, inner_ref, inner_code, t_ref, w_ref, *m_refs
    ):
        core = lax.axis_index("space") & 1
        start = pl.program_id(0) * STEP

        def beside(a_ref, b_ref, j):
            a = [a_ref[j, i].astype(F32) for i in range(2)]
            b = [b_ref[j, i].astype(F32) for i in range(2)]
            below = [jnp.where(core == 0, a[i], b[i]) for i in range(2)]
            above = [jnp.where(core == 0, b[i], a[i]) for i in range(2)]
            return {-2: below[0], -1: below[1], 4: above[0], 5: above[1]}

        codes = beside(away_code, inner_code, 0)
        codes.update({i: l_ref[i].astype(F32) for i in range(4)})

        def one(j, _):
            cells = beside(away_ref, inner_ref, j)
            cells.update({i: d_ref[j, i] for i in range(4)})
            values = update(cells, codes, h_ref[start + j], c_ref[start + j], range(4))
            for i, value in enumerate(values):
                t_ref[j, i] = value
            return 0

        lax.fori_loop(0, STEP, one, 0, unroll=4)
        for m_ref, layers in zip(m_refs, BLOCKS, strict=True):
            for place, i in enumerate(layers):
                turned = jnp.swapaxes(t_ref[:, i], 0, 1)
                for y in range(8):
                    m_ref[:, pl.ds(place * 1024 + y * 128, 128)] = turned[y].astype(BF16)

        @pl.when(pl.program_id(0) % 2 == 0)
        def _():
            w_ref[0] = t_ref[0].astype(BF16)

    halo = pl.BlockSpec((STEP, 2, 8, 128), lambda i: (i, 0, 0, 0))
    code = pl.BlockSpec((1, 2, 8, 128), lambda i: (rows, 0, 0, 0))
    full = pl.BlockSpec((STEP, 4, 8, 128), lambda i: (i, 0, 0, 0))
    outs = pl.pallas_call(
        kernel,
        grid=(rows // STEP,),
        out_shape=(shape(density.shape, F32), shape((2, 4, 8, 128), BF16))
        + tuple(shape((rows, 1024 * len(layers)), BF16) for layers in BLOCKS),
        in_specs=[
            SMEM,
            SMEM,
            full,
            pl.BlockSpec((4, 8, 128), lambda i: (0, 0, 0)),
            halo,
            code,
            halo,
            code,
        ],
        out_specs=(full, pl.BlockSpec((1, 4, 8, 128), lambda i: (i // 2, 0, 0, 0)))
        + tuple(pl.BlockSpec((STEP, 1024 * len(layers)), lambda i: (i, 0)) for layers in BLOCKS),
        cost_estimate=pl.CostEstimate(flops=4 << 20, bytes_accessed=6 << 20, transcendentals=0),
        name="transport",
    )(heading, courant, density, limiter, away, away, inner, inner)
    return outs[0], outs[1], outs[2:]


ORDER = [(0, 0), (0, 1), (3, 0), (3, 1), (1, 0), (1, 1), (2, 0), (2, 1)]


def weight_rows():
    vel, space = lax.axis_index("vel"), lax.axis_index("space")
    y, z = vel >> 1, vel & 1
    x, h, c = space >> 2, (space >> 1) & 1, space & 1
    rows = []
    for dc in range(2):
        for dx, dh in ORDER:
            v = (((x + dx) & 3) << 1) + (h ^ dh)
            rows.append(((((v >> 1) - y) & 3) << 2) + (((v & 1) ^ z) << 1) + (c ^ dc))
    return y, rows


def collide(layer, place, pieces, blocks, weights):
    cells = 1024
    tile = 512
    columns = pl.ds(place * cells, cells)
    def kernel(*refs):
        w_parts = refs[:4]
        slabs = refs[4:12]
        parts = refs[12:16]
        mine_ref, other_ref, k_ref, m_ref, w_ref, sem_k, sem_m = refs[16:]
        y, places = weight_rows()
        loads = []
        for d in range(4):
            at = pl.multiple_of(((y + d) & 3) * 128, 128)
            loads.append(
                pltpu.make_async_copy(
                    parts[d].at[:, columns], m_ref.at[pl.ds(at, 128)], sem_m.at[d]
                )
            )
        for i in range(8):
            loads.append(
                pltpu.make_async_copy(slabs[i], k_ref.at[pl.ds(512 * i, 512)], sem_k.at[i])
            )
        for load in loads:
            load.start()
        for d in range(4):
            w_ref[4 * d : 4 * d + 4] = w_parts[d][:, layer].astype(F32)
        for load in loads[:4]:
            load.wait()
        for t in range(cells // tile):
            cols = pl.ds(t * tile, tile)
            moved = m_ref[:, cols]
            total = jnp.zeros((256, tile), F32)
            for s in range(SLICES):
                if t == 0 and s % 2 == 0:
                    loads[4 + s // 2].wait()
                product = jnp.dot(
                    k_ref[s * 256 : (s + 1) * 256], moved, preferred_element_type=F32
                )
                lines = [w_ref[places[s], pl.ds(t * 4 + i, 1), :] for i in range(tile // 128)]
                total = total + jnp.concatenate(lines, 1) * product
            mine_ref[:, cols] = total[:128]
            other_ref[:, cols] = total[128:].astype(BF16)

    return pl.pallas_call(
        kernel,
        out_shape=(shape((128, cells), F32), shape((128, cells), BF16)),
        in_specs=[VMEM] * 4 + [ANY] * 12,
        out_specs=(VMEM, VMEM),
        scratch_shapes=[
            pltpu.VMEM((SLICES * 256, 512), BF16),
            pltpu.VMEM((512, cells), BF16),
            pltpu.VMEM((SLICES, 8, 128), F32),
            pltpu.SemaphoreType.DMA((8,)),
            pltpu.SemaphoreType.DMA((4,)),
        ],
        compiler_params=pltpu.CompilerParams(vmem_limit_bytes=28 << 20),
        cost_estimate=pl.CostEstimate(
            flops=2 * SLICES * 256 * 512 * cells, bytes_accessed=6 << 20, transcendentals=0
        ),
        name="collide",
    )(*weights, *pieces, *blocks)


def combine(layer, mine, got, result):
    step = 64

    def kernel(a_ref, b_ref, *refs):
        o_ref = refs[-1]
        total = a_ref[...] + b_ref[...].astype(F32)
        lines = jnp.stack([total[:, y * 128 : (y + 1) * 128] for y in range(8)], 0)
        o_ref[:, 0] = jnp.swapaxes(lines, 0, 1)

    block = pl.BlockSpec((step, 1024), lambda i: (i, 0))
    given = [] if result is None else [result]
    return pl.pallas_call(
        kernel,
        grid=(128 // step,),
        out_shape=shape((128, 4, 8, 128), F32),
        in_specs=[block, block] + [ANY] * len(given),
        out_specs=pl.BlockSpec((step, 1, 8, 128), lambda i: (i, layer, 0, 0)),
        input_output_aliases={2: 0} if given else {},
        cost_estimate=pl.CostEstimate(flops=1 << 17, bytes_accessed=5 << 18, transcendentals=0),
        name="combine",
    )(mine, got, *given)


def local(density, limiter, heading, courant, kernel_slices):
    size = lax.axis_size("space")
    beside = [(i, i + 1) for i in range(1, size - 1, 2)]
    beside = beside + [(j, i) for i, j in beside]

    own_slice = split_slice(kernel_slices[0])
    partner = shift(own_slice, dz=1)
    payload, inner = pack(after(density, own_slice), limiter)
    away = lax.ppermute(payload, "space", beside)
    inner = shift(inner, dc=1)

    crossing = jnp.concatenate([partner[128:], own_slice[:128]], 0)
    cross = shift(after(crossing, payload), dz=1, dh=1)
    base = jnp.concatenate([own_slice[128:], partner[:128], after(cross, inner)], 0)
    pieces = [base, shift(base, dx=1), shift(base, dx=-1), shift(base, dx=2)]
    pieces = pieces + [shift(p, dc=1) for p in pieces]

    away = after(away, pieces[4])
    transported, own, blocks = transport(density, limiter, heading, courant, away, inner)
    rows = jnp.concatenate([own, shift(own, dz=1)], 0)
    weights = [rows, shift(rows, dy=-1), shift(rows, dy=2), shift(rows, dy=1)]

    results, got, column = [None], [], ()
    for layers, block in zip(BLOCKS, blocks, strict=True):
        block = after(block, *column[1:])
        column = [block, shift(block, dy=-1), shift(block, dy=2), shift(block, dy=1)]
        for place, layer in enumerate(layers):
            mine, other = collide(layer, place, pieces, column, weights)
            weights = after(weights, mine, *got[-1:], *results[1:][-1:])
            got.append(shift(other, dz=1))
            results.append(combine(layer, mine, got[-1], results[-1]))
    return transported, results[-1]


def solution(mesh):
    return jax.shard_map(
        local,
        mesh=mesh,
        in_specs=(
            P("vel", "space", None, None),
            P("space", None, None),
            P("vel"),
            P("vel"),
            P("space", None, "vel"),
        ),
        out_specs=(P("vel", "space", None, None), P("vel", "space", None, None)),
        check_vma=False,
    )
```

```python
import jax
import jax.numpy as jnp
from jax import lax
from jax.experimental import pallas as pl
from jax.experimental.pallas import tpu as pltpu
from jax.sharding import PartitionSpec as P

SLICES = 16
BLOCKS = ((1, 2), (0, 3))
BOTH = ("vel", "space")
FLAT = [
    (y, z, x, h, c)
    for y in range(4)
    for z in range(2)
    for x in range(4)
    for h in range(2)
    for c in range(2)
]
BF16, F32 = jnp.bfloat16, jnp.float32
ANY = pl.BlockSpec(memory_space=pl.ANY)
VMEM = pl.BlockSpec(memory_space=pltpu.VMEM)
SMEM = pl.BlockSpec(memory_space=pltpu.SMEM)


def rank(y, z, x, h, c):
    return ((y % 4) * 2 + z) * 16 + (x % 4) * 4 + h * 2 + c


def shift(value, dy=0, dz=0, dx=0, dh=0, dc=0):
    pairs = [
        (rank(y, z, x, h, c), rank(y + dy, z ^ dz, x + dx, h ^ dh, c ^ dc)) for y, z, x, h, c in FLAT
    ]
    return lax.ppermute(value, BOTH, pairs)


def after(value, *earlier):
    return lax.optimization_barrier((value, earlier))[0]


def shape(dims, dtype):
    return jax.ShapeDtypeStruct(dims, dtype)


def pack(density, limiter):
    rows = density.shape[0]

    def kernel(d_ref, l_ref, first_ref, second_ref, inner_ref):
        core = lax.axis_index("space") & 1

        def fill(outer, following, pair):
            first_ref[:rows] = d_ref[:, outer].astype(BF16)
            first_ref[rows] = l_ref[outer].astype(F32).astype(BF16)
            for i in range(2):
                first_ref[rows + 1 + i] = d_ref[64 * i, following].astype(BF16)
            second_ref[...] = d_ref[:, following].astype(BF16)
            inner_ref[:rows] = d_ref[:, pair : pair + 2].astype(BF16)
            inner_ref[rows] = l_ref[pair : pair + 2].astype(F32).astype(BF16)

        @pl.when(core == 1)
        def _():
            fill(3, 2, 0)

        @pl.when(core == 0)
        def _():
            fill(0, 1, 2)

    dims = density.shape[2:]
    return pl.pallas_call(
        kernel,
        out_shape=(
            shape((rows + 3, *dims), BF16),
            shape((rows, *dims), BF16),
            shape((rows + 1, 2, *dims), BF16),
        ),
        in_specs=[VMEM, VMEM],
        out_specs=(VMEM, VMEM, VMEM),
        name="pack",
    )(density, limiter)


def split_slice(kernel_slice):
    def kernel(k_ref, o_ref):
        z = lax.axis_index("vel") & 1
        for y in range(4):
            cols = pl.ds(y * 128, 128)
            o_ref[:128, cols] = k_ref[y, 1 - z].astype(F32).T.astype(BF16)
            o_ref[128:, cols] = k_ref[y, z].astype(F32).T.astype(BF16)

    return pl.pallas_call(
        kernel, out_shape=shape((256, 512), BF16), in_specs=[VMEM], out_specs=VMEM, name="split_slice"
    )(kernel_slice.reshape(4, 2, 128, 128))


def update(cells, codes, ahead, number, layers):
    half = 0.5 * (2 * ahead - 1).astype(F32)
    forward = jnp.full((8, 128), ahead, jnp.int32) == 1
    rebuilt = {}
    for i in sorted({i + d for i in layers for d in (-1, 0, 1)}):
        left, right = cells[i] - cells[i - 1], cells[i + 1] - cells[i]
        small = jnp.where(left > 0, jnp.minimum(left, right), jnp.maximum(left, right))
        small = jnp.where(left * right > 0, small, 0.0)
        slope = jnp.where(
            codes[i] == 1, small, jnp.where(codes[i] == 2, 0.5 * (left + right), 0.0)
        )
        rebuilt[i] = cells[i] + half * slope
    return [
        cells[i] - number * (rebuilt[i] - jnp.where(forward, rebuilt[i - 1], rebuilt[i + 1]))
        for i in layers
    ]


STEP = 32


def transport_specs(rows):
    return [
        SMEM,
        SMEM,
        pl.BlockSpec((STEP, 4, 8, 128), lambda i: (i, 0, 0, 0)),
        pl.BlockSpec((4, 8, 128), lambda i: (0, 0, 0)),
        pl.BlockSpec((STEP, 8, 128), lambda i: (i, 0, 0)),
        pl.BlockSpec((1, 8, 128), lambda i: (rows, 0, 0)),
        pl.BlockSpec((STEP, 2, 8, 128), lambda i: (i, 0, 0, 0)),
        pl.BlockSpec((1, 2, 8, 128), lambda i: (rows, 0, 0, 0)),
    ]


def outer_codes(core, l_ref, first_code, inner_code):
    codes = {i: l_ref[i].astype(F32) for i in range(4)}
    codes[-1] = jnp.where(core == 0, first_code[0].astype(F32), inner_code[0, 1].astype(F32))
    codes[4] = jnp.where(core == 0, inner_code[0, 0].astype(F32), first_code[0].astype(F32))
    return codes


def neighbours(core, j, first_ref, inner_ref, second=None):
    a, b = inner_ref[j, 0].astype(F32), inner_ref[j, 1].astype(F32)
    first = first_ref[j].astype(F32)
    cells = {-1: jnp.where(core == 0, first, b), 4: jnp.where(core == 0, a, first)}
    if second is not None:
        second = second.astype(F32)
        cells[-2] = jnp.where(core == 0, second, a)
        cells[5] = jnp.where(core == 0, b, second)
    return cells


def flatten(m_ref, t_ref, places):
    for place, i in enumerate(places):
        turned = jnp.swapaxes(t_ref[:, i], 0, 1)
        for y in range(8):
            m_ref[:, pl.ds(place * 1024 + y * 128, 128)] = turned[y].astype(BF16)


def transport_inner(density, limiter, heading, courant, first, inner):
    rows = density.shape[0]

    def kernel(
        h_ref, c_ref, d_ref, l_ref, first_ref, first_code, inner_ref, inner_code, next_ref, m_ref, w_ref, t_ref
    ):
        core = lax.axis_index("space") & 1
        start = pl.program_id(0) * STEP
        codes = outer_codes(core, l_ref, first_code, inner_code)

        def one(j, _):
            cells = {i: d_ref[j, i] for i in range(4)}
            cells.update(neighbours(core, j, first_ref, inner_ref))
            values = update(cells, codes, h_ref[start + j], c_ref[start + j], (1, 2))
            for i, value in enumerate(values):
                t_ref[j, i] = value
            return 0

        lax.fori_loop(0, STEP, one, 0, unroll=4)
        flatten(m_ref, t_ref, (0, 1))

        @pl.when(pl.program_id(0) % 2 == 0)
        def _():
            cells = {i: d_ref[0, i] for i in range(4)}
            cells.update(neighbours(core, 0, first_ref, inner_ref, next_ref[0]))
            values = update(cells, codes, h_ref[start], c_ref[start], range(4))
            for i, value in enumerate(values):
                w_ref[0, i] = value.astype(BF16)

    return pl.pallas_call(
        kernel,
        grid=(rows // STEP,),
        out_shape=(shape((rows, 2048), BF16), shape((2, 4, 8, 128), BF16)),
        in_specs=transport_specs(rows)
        + [pl.BlockSpec((1, 8, 128), lambda i: (rows + 1 + i // 2, 0, 0))],
        out_specs=(
            pl.BlockSpec((STEP, 2048), lambda i: (i, 0)),
            pl.BlockSpec((1, 4, 8, 128), lambda i: (i // 2, 0, 0, 0)),
        ),
        scratch_shapes=[pltpu.VMEM((STEP, 2, 8, 128), F32)],
        cost_estimate=pl.CostEstimate(flops=2 << 20, bytes_accessed=3 << 20, transcendentals=0),
        name="transport_inner",
    )(heading, courant, density, limiter, first, first, inner, inner, first)


def transport(density, limiter, heading, courant, first, second, inner):
    rows = density.shape[0]

    def kernel(
        h_ref, c_ref, d_ref, l_ref, first_ref, first_code, inner_ref, inner_code, next_ref, t_ref, m_ref
    ):
        core = lax.axis_index("space") & 1
        start = pl.program_id(0) * STEP
        codes = outer_codes(core, l_ref, first_code, inner_code)

        def one(j, _):
            cells = {i: d_ref[j, i] for i in range(4)}
            cells.update(neighbours(core, j, first_ref, inner_ref, next_ref[j]))
            values = update(cells, codes, h_ref[start + j], c_ref[start + j], range(4))
            for i, value in enumerate(values):
                t_ref[j, i] = value
            return 0

        lax.fori_loop(0, STEP, one, 0, unroll=4)
        flatten(m_ref, t_ref, (0, 3))

    return pl.pallas_call(
        kernel,
        grid=(rows // STEP,),
        out_shape=(shape(density.shape, F32), shape((rows, 2048), BF16)),
        in_specs=transport_specs(rows) + [pl.BlockSpec((STEP, 8, 128), lambda i: (i, 0, 0))],
        out_specs=(
            pl.BlockSpec((STEP, 4, 8, 128), lambda i: (i, 0, 0, 0)),
            pl.BlockSpec((STEP, 2048), lambda i: (i, 0)),
        ),
        cost_estimate=pl.CostEstimate(flops=4 << 20, bytes_accessed=6 << 20, transcendentals=0),
        name="transport",
    )(heading, courant, density, limiter, first, first, inner, inner, second)


ORDER = [(0, 0), (0, 1), (3, 0), (3, 1), (1, 0), (1, 1), (2, 0), (2, 1)]


def weight_rows():
    vel, space = lax.axis_index("vel"), lax.axis_index("space")
    y, z = vel >> 1, vel & 1
    x, h, c = space >> 2, (space >> 1) & 1, space & 1
    rows = []
    for dc in range(2):
        for dx, dh in ORDER:
            v = (((x + dx) & 3) << 1) + (h ^ dh)
            rows.append(((((v >> 1) - y) & 3) << 2) + (((v & 1) ^ z) << 1) + (c ^ dc))
    return y, rows


def collide(layer, place, pieces, blocks, weights):
    cells = 1024
    tile = 512
    columns = pl.ds(place * cells, cells)
    targets = [(0, 0, 128), (1, 0, 128), (3, 0, 128), (2, 0, 64), (2, 64, 64)]

    def kernel(*refs):
        w_parts = refs[:4]
        slabs = refs[4:14]
        parts = refs[14:19]
        mine_ref, other_ref, k_ref, m_ref, w_ref, sem_k, sem_m = refs[19:]
        y, places = weight_rows()
        loads = []
        for i, (d, skip, n) in enumerate(targets):
            at = pl.multiple_of(((y + d) & 3) * 128 + skip, 64)
            loads.append(
                pltpu.make_async_copy(
                    parts[i].at[:, columns], m_ref.at[pl.ds(at, n)], sem_m.at[i]
                )
            )
        row, starts = 0, []
        for i in range(10):
            n = slabs[i].shape[0]
            loads.append(pltpu.make_async_copy(slabs[i], k_ref.at[pl.ds(row, n)], sem_k.at[i]))
            starts.append(row // 256)
            row += n
        for load in loads:
            load.start()
        for d in range(4):
            w_ref[4 * d : 4 * d + 4] = w_parts[d][:, layer].astype(F32)
        for load in loads[:5]:
            load.wait()
        for t in range(cells // tile):
            cols = pl.ds(t * tile, tile)
            moved = m_ref[:, cols]
            total = jnp.zeros((256, tile), F32)
            for s in range(SLICES):
                if t == 0 and s in starts:
                    loads[5 + starts.index(s)].wait()
                product = jnp.dot(
                    k_ref[s * 256 : (s + 1) * 256], moved, preferred_element_type=F32
                )
                lines = [w_ref[places[s], pl.ds(t * 4 + i, 1), :] for i in range(tile // 128)]
                total = total + jnp.concatenate(lines, 1) * product
            mine_ref[:, cols] = total[:128]
            other_ref[:, cols] = total[128:].astype(BF16)

    return pl.pallas_call(
        kernel,
        out_shape=(shape((128, cells), F32), shape((128, cells), BF16)),
        in_specs=[VMEM] * 4 + [ANY] * 15,
        out_specs=(VMEM, VMEM),
        scratch_shapes=[
            pltpu.VMEM((SLICES * 256, 512), BF16),
            pltpu.VMEM((512, cells), BF16),
            pltpu.VMEM((SLICES, 8, 128), F32),
            pltpu.SemaphoreType.DMA((10,)),
            pltpu.SemaphoreType.DMA((5,)),
        ],
        compiler_params=pltpu.CompilerParams(vmem_limit_bytes=28 << 20),
        cost_estimate=pl.CostEstimate(
            flops=2 * SLICES * 256 * 512 * cells, bytes_accessed=6 << 20, transcendentals=0
        ),
        name="collide",
    )(*weights, *pieces, *blocks)


def combine(layer, mine, got, result):
    step = 64

    def kernel(a_ref, b_ref, *refs):
        o_ref = refs[-1]
        total = a_ref[...] + b_ref[...].astype(F32)
        lines = jnp.stack([total[:, y * 128 : (y + 1) * 128] for y in range(8)], 0)
        o_ref[:, 0] = jnp.swapaxes(lines, 0, 1)

    block = pl.BlockSpec((step, 1024), lambda i: (i, 0))
    given = [] if result is None else [result]
    return pl.pallas_call(
        kernel,
        grid=(128 // step,),
        out_shape=shape((128, 4, 8, 128), F32),
        in_specs=[block, block] + [ANY] * len(given),
        out_specs=pl.BlockSpec((step, 1, 8, 128), lambda i: (i, layer, 0, 0)),
        input_output_aliases={2: 0} if given else {},
        cost_estimate=pl.CostEstimate(flops=1 << 17, bytes_accessed=5 << 18, transcendentals=0),
        name="combine",
    )(mine, got, *given)


def local(density, limiter, heading, courant, kernel_slices):
    size = lax.axis_size("space")
    beside = [(i, i + 1) for i in range(1, size - 1, 2)]
    beside = beside + [(j, i) for i, j in beside]

    own_slice = split_slice(kernel_slices[0])
    partner = shift(own_slice, dz=1)
    first, second, inner = pack(after(density, own_slice), limiter)
    first = lax.ppermute(first, "space", beside)
    inner = shift(inner, dc=1)

    crossing = jnp.concatenate([partner[128:], own_slice[:128]], 0)
    cross = shift(crossing, dz=1, dh=1)
    first = after(first, crossing)
    second = lax.ppermute(after(second, first), "space", beside)
    block, own = transport_inner(density, limiter, heading, courant, first, inner)

    base = jnp.concatenate([own_slice[128:], partner[:128], after(cross, block)], 0)
    swapped = [shift(base, dc=1)]
    block = after(block, swapped[0])
    before, behind = shift(block, dy=1), shift(block, dy=-1)
    one, three, before, behind = after(
        (shift(base, dx=1), shift(base, dx=-1), before, behind)
    )
    pieces = [base, one, three, shift(one[:256], dx=1), shift(three[256:], dx=-1)]
    pieces = pieces + swapped + [shift(p, dc=1) for p in pieces[1:]]
    inside = [block, behind, before, shift(before[:64], dy=1), shift(behind[64:], dy=-1)]

    rows = after(jnp.concatenate([own, shift(own, dz=1)], 0), before)
    weights = [rows, shift(rows, dy=-1), shift(rows, dy=2), shift(rows, dy=1)]
    second = after(second, before)
    transported, block = transport(density, limiter, heading, courant, first, second, inner)
    before, behind = shift(block, dy=1), shift(block, dy=-1)
    across = shift(block, dy=2)
    outside = [block, behind, before, across[:64], across[64:]]

    results, got = [None], []
    for layers, blocks in zip(BLOCKS, (inside, outside), strict=True):
        for place, layer in enumerate(layers):
            mine, other = collide(layer, place, pieces, blocks, weights)
            weights = after(weights, mine, *got[-1:], *results[1:][-1:])
            got.append(shift(other, dz=1))
            results.append(combine(layer, mine, got[-1], results[-1]))
    return transported, results[-1]


def solution(mesh):
    return jax.shard_map(
        local,
        mesh=mesh,
        in_specs=(
            P("vel", "space", None, None),
            P("space", None, None),
            P("vel"),
            P("vel"),
            P("space", None, "vel"),
        ),
        out_specs=(P("vel", "space", None, None), P("vel", "space", None, None)),
        check_vma=False,
    )
```

```python
import jax
import jax.numpy as jnp
from jax import lax
from jax.experimental import pallas as pl
from jax.experimental.pallas import tpu as pltpu
from jax.sharding import PartitionSpec as P

SLICES = 16
BLOCKS = ((1, 2), (0, 3))
BOTH = ("vel", "space")
FLAT = [
    (y, z, x, h, c)
    for y in range(4)
    for z in range(2)
    for x in range(4)
    for h in range(2)
    for c in range(2)
]
BF16, F32 = jnp.bfloat16, jnp.float32
ANY = pl.BlockSpec(memory_space=pl.ANY)
VMEM = pl.BlockSpec(memory_space=pltpu.VMEM)
SMEM = pl.BlockSpec(memory_space=pltpu.SMEM)


def rank(y, z, x, h, c):
    return ((y % 4) * 2 + z) * 16 + (x % 4) * 4 + h * 2 + c


def shift(value, dy=0, dz=0, dx=0, dh=0, dc=0):
    pairs = [
        (rank(y, z, x, h, c), rank(y + dy, z ^ dz, x + dx, h ^ dh, c ^ dc)) for y, z, x, h, c in FLAT
    ]
    return lax.ppermute(value, BOTH, pairs)


def after(value, *earlier):
    return lax.optimization_barrier((value, earlier))[0]


def shape(dims, dtype):
    return jax.ShapeDtypeStruct(dims, dtype)


def pack(density, limiter):
    rows = density.shape[0]

    def kernel(d_ref, l_ref, first_ref, second_ref, inner_ref):
        core = lax.axis_index("space") & 1

        def fill(outer, following, pair):
            first_ref[:rows] = d_ref[:, outer].astype(BF16)
            first_ref[rows] = l_ref[outer].astype(F32).astype(BF16)
            for i in range(2):
                first_ref[rows + 1 + i] = d_ref[64 * i, following].astype(BF16)
            second_ref[...] = d_ref[:, following].astype(BF16)
            inner_ref[:rows] = d_ref[:, pair : pair + 2].astype(BF16)
            inner_ref[rows] = l_ref[pair : pair + 2].astype(F32).astype(BF16)

        @pl.when(core == 1)
        def _():
            fill(3, 2, 0)

        @pl.when(core == 0)
        def _():
            fill(0, 1, 2)

    dims = density.shape[2:]
    return pl.pallas_call(
        kernel,
        out_shape=(
            shape((rows + 3, *dims), BF16),
            shape((rows, *dims), BF16),
            shape((rows + 1, 2, *dims), BF16),
        ),
        in_specs=[VMEM, VMEM],
        out_specs=(VMEM, VMEM, VMEM),
        name="pack",
    )(density, limiter)


def split_slice(kernel_slice):
    def kernel(k_ref, o_ref):
        z = lax.axis_index("vel") & 1
        for y in range(4):
            cols = pl.ds(y * 128, 128)
            o_ref[:128, cols] = k_ref[y, 1 - z].astype(F32).T.astype(BF16)
            o_ref[128:, cols] = k_ref[y, z].astype(F32).T.astype(BF16)

    return pl.pallas_call(
        kernel, out_shape=shape((256, 512), BF16), in_specs=[VMEM], out_specs=VMEM, name="split_slice"
    )(kernel_slice.reshape(4, 2, 128, 128))


def update(cells, codes, ahead, number, layers):
    half = 0.5 * (2 * ahead - 1).astype(F32)
    forward = jnp.full((8, 128), ahead, jnp.int32) == 1
    rebuilt = {}
    for i in sorted({i + d for i in layers for d in (-1, 0, 1)}):
        left, right = cells[i] - cells[i - 1], cells[i + 1] - cells[i]
        small = jnp.where(left > 0, jnp.minimum(left, right), jnp.maximum(left, right))
        small = jnp.where(left * right > 0, small, 0.0)
        slope = jnp.where(
            codes[i] == 1, small, jnp.where(codes[i] == 2, 0.5 * (left + right), 0.0)
        )
        rebuilt[i] = cells[i] + half * slope
    return [
        cells[i] - number * (rebuilt[i] - jnp.where(forward, rebuilt[i - 1], rebuilt[i + 1]))
        for i in layers
    ]


STEP = 32


def transport_specs(rows):
    return [
        SMEM,
        SMEM,
        pl.BlockSpec((STEP, 4, 8, 128), lambda i: (i, 0, 0, 0)),
        pl.BlockSpec((4, 8, 128), lambda i: (0, 0, 0)),
        pl.BlockSpec((STEP, 8, 128), lambda i: (i, 0, 0)),
        pl.BlockSpec((1, 8, 128), lambda i: (rows, 0, 0)),
        pl.BlockSpec((STEP, 2, 8, 128), lambda i: (i, 0, 0, 0)),
        pl.BlockSpec((1, 2, 8, 128), lambda i: (rows, 0, 0, 0)),
    ]


def outer_codes(core, l_ref, first_code, inner_code):
    codes = {i: l_ref[i].astype(F32) for i in range(4)}
    codes[-1] = jnp.where(core == 0, first_code[0].astype(F32), inner_code[0, 1].astype(F32))
    codes[4] = jnp.where(core == 0, inner_code[0, 0].astype(F32), first_code[0].astype(F32))
    return codes


def neighbours(core, j, first_ref, inner_ref, second=None):
    a, b = inner_ref[j, 0].astype(F32), inner_ref[j, 1].astype(F32)
    first = first_ref[j].astype(F32)
    cells = {-1: jnp.where(core == 0, first, b), 4: jnp.where(core == 0, a, first)}
    if second is not None:
        second = second.astype(F32)
        cells[-2] = jnp.where(core == 0, second, a)
        cells[5] = jnp.where(core == 0, b, second)
    return cells


def flatten(m_ref, t_ref, places):
    for place, i in enumerate(places):
        turned = jnp.swapaxes(t_ref[:, i], 0, 1)
        for y in range(8):
            m_ref[:, pl.ds(place * 1024 + y * 128, 128)] = turned[y].astype(BF16)


def transport_inner(density, limiter, heading, courant, first, inner):
    rows = density.shape[0]

    def kernel(
        h_ref, c_ref, d_ref, l_ref, first_ref, first_code, inner_ref, inner_code, next_ref, m_ref, w_ref, t_ref
    ):
        core = lax.axis_index("space") & 1
        start = pl.program_id(0) * STEP
        codes = outer_codes(core, l_ref, first_code, inner_code)

        def one(j, _):
            cells = {i: d_ref[j, i] for i in range(4)}
            cells.update(neighbours(core, j, first_ref, inner_ref))
            values = update(cells, codes, h_ref[start + j], c_ref[start + j], (1, 2))
            for i, value in enumerate(values):
                t_ref[j, i] = value
            return 0

        lax.fori_loop(0, STEP, one, 0, unroll=4)
        flatten(m_ref, t_ref, (0, 1))

        @pl.when(pl.program_id(0) % 2 == 0)
        def _():
            cells = {i: d_ref[0, i] for i in range(4)}
            cells.update(neighbours(core, 0, first_ref, inner_ref, next_ref[0]))
            values = update(cells, codes, h_ref[start], c_ref[start], range(4))
            for i, value in enumerate(values):
                w_ref[0, i] = value.astype(BF16)

    return pl.pallas_call(
        kernel,
        grid=(rows // STEP,),
        out_shape=(shape((rows, 2048), BF16), shape((2, 4, 8, 128), BF16)),
        in_specs=transport_specs(rows)
        + [pl.BlockSpec((1, 8, 128), lambda i: (rows + 1 + i // 2, 0, 0))],
        out_specs=(
            pl.BlockSpec((STEP, 2048), lambda i: (i, 0)),
            pl.BlockSpec((1, 4, 8, 128), lambda i: (i // 2, 0, 0, 0)),
        ),
        scratch_shapes=[pltpu.VMEM((STEP, 2, 8, 128), F32)],
        cost_estimate=pl.CostEstimate(flops=2 << 20, bytes_accessed=3 << 20, transcendentals=0),
        name="transport_inner",
    )(heading, courant, density, limiter, first, first, inner, inner, first)


def transport(density, limiter, heading, courant, first, second, inner):
    rows = density.shape[0]

    def kernel(
        h_ref, c_ref, d_ref, l_ref, first_ref, first_code, inner_ref, inner_code, next_ref, t_ref, m_ref
    ):
        core = lax.axis_index("space") & 1
        start = pl.program_id(0) * STEP
        codes = outer_codes(core, l_ref, first_code, inner_code)

        def one(j, _):
            cells = {i: d_ref[j, i] for i in range(4)}
            cells.update(neighbours(core, j, first_ref, inner_ref, next_ref[j]))
            values = update(cells, codes, h_ref[start + j], c_ref[start + j], range(4))
            for i, value in enumerate(values):
                t_ref[j, i] = value
            return 0

        lax.fori_loop(0, STEP, one, 0, unroll=4)
        flatten(m_ref, t_ref, (0, 3))

    return pl.pallas_call(
        kernel,
        grid=(rows // STEP,),
        out_shape=(shape(density.shape, F32), shape((rows, 2048), BF16)),
        in_specs=transport_specs(rows) + [pl.BlockSpec((STEP, 8, 128), lambda i: (i, 0, 0))],
        out_specs=(
            pl.BlockSpec((STEP, 4, 8, 128), lambda i: (i, 0, 0, 0)),
            pl.BlockSpec((STEP, 2048), lambda i: (i, 0)),
        ),
        cost_estimate=pl.CostEstimate(flops=4 << 20, bytes_accessed=6 << 20, transcendentals=0),
        name="transport",
    )(heading, courant, density, limiter, first, first, inner, inner, second)


ORDER = [(0, 0), (0, 1), (3, 0), (3, 1), (1, 0), (1, 1), (2, 0), (2, 1)]


def weight_rows():
    vel, space = lax.axis_index("vel"), lax.axis_index("space")
    y, z = vel >> 1, vel & 1
    x, h, c = space >> 2, (space >> 1) & 1, space & 1
    rows = []
    for dc in range(2):
        for dx, dh in ORDER:
            v = (((x + dx) & 3) << 1) + (h ^ dh)
            rows.append(((((v >> 1) - y) & 3) << 2) + (((v & 1) ^ z) << 1) + (c ^ dc))
    return y, rows


def collide(layer, place, pieces, blocks, weights):
    cells = 1024
    tile = 512
    columns = pl.ds(place * cells, cells)
    targets = [(0, 0, 128), (1, 0, 128), (3, 0, 128), (2, 0, 64), (2, 64, 64)]

    def kernel(*refs):
        w_parts = refs[:4]
        slabs = refs[4:14]
        parts = refs[14:19]
        mine_ref, other_ref, k_ref, m_ref, w_ref, sem_k, sem_m = refs[19:]
        y, places = weight_rows()
        loads = []
        for i, (d, skip, n) in enumerate(targets):
            at = pl.multiple_of(((y + d) & 3) * 128 + skip, 64)
            loads.append(
                pltpu.make_async_copy(
                    parts[i].at[:, columns], m_ref.at[pl.ds(at, n)], sem_m.at[i]
                )
            )
        row, starts = 0, []
        for i in range(10):
            n = slabs[i].shape[0]
            loads.append(pltpu.make_async_copy(slabs[i], k_ref.at[pl.ds(row, n)], sem_k.at[i]))
            starts.append(row // 256)
            row += n
        for load in loads:
            load.start()
        for d in range(4):
            w_ref[4 * d : 4 * d + 4] = w_parts[d][:, layer].astype(F32)
        for load in loads[:5]:
            load.wait()
        for t in range(cells // tile):
            cols = pl.ds(t * tile, tile)
            moved = m_ref[:, cols]
            total = jnp.zeros((256, tile), F32)
            for s in range(SLICES):
                if t == 0 and s in starts:
                    loads[5 + starts.index(s)].wait()
                product = jnp.dot(
                    k_ref[s * 256 : (s + 1) * 256], moved, preferred_element_type=F32
                )
                lines = [w_ref[places[s], pl.ds(t * 4 + i, 1), :] for i in range(tile // 128)]
                total = total + jnp.concatenate(lines, 1) * product
            mine_ref[:, cols] = total[:128]
            other_ref[:, cols] = total[128:].astype(BF16)

    return pl.pallas_call(
        kernel,
        out_shape=(shape((128, cells), F32), shape((128, cells), BF16)),
        in_specs=[VMEM] * 4 + [ANY] * 15,
        out_specs=(VMEM, VMEM),
        scratch_shapes=[
            pltpu.VMEM((SLICES * 256, 512), BF16),
            pltpu.VMEM((512, cells), BF16),
            pltpu.VMEM((SLICES, 8, 128), F32),
            pltpu.SemaphoreType.DMA((10,)),
            pltpu.SemaphoreType.DMA((5,)),
        ],
        compiler_params=pltpu.CompilerParams(vmem_limit_bytes=28 << 20),
        cost_estimate=pl.CostEstimate(
            flops=2 * SLICES * 256 * 512 * cells, bytes_accessed=6 << 20, transcendentals=0
        ),
        name="collide",
    )(*weights, *pieces, *blocks)


def combine(layer, mine, got, result):
    step = 64

    def kernel(a_ref, b_ref, *refs):
        o_ref = refs[-1]
        total = a_ref[...] + b_ref[...].astype(F32)
        lines = jnp.stack([total[:, y * 128 : (y + 1) * 128] for y in range(8)], 0)
        o_ref[:, 0] = jnp.swapaxes(lines, 0, 1)

    block = pl.BlockSpec((step, 1024), lambda i: (i, 0))
    given = [] if result is None else [result]
    return pl.pallas_call(
        kernel,
        grid=(128 // step,),
        out_shape=shape((128, 4, 8, 128), F32),
        in_specs=[block, block] + [ANY] * len(given),
        out_specs=pl.BlockSpec((step, 1, 8, 128), lambda i: (i, layer, 0, 0)),
        input_output_aliases={2: 0} if given else {},
        cost_estimate=pl.CostEstimate(flops=1 << 17, bytes_accessed=5 << 18, transcendentals=0),
        name="combine",
    )(mine, got, *given)


def local(density, limiter, heading, courant, kernel_slices):
    size = lax.axis_size("space")
    beside = [(i, i + 1) for i in range(1, size - 1, 2)]
    beside = beside + [(j, i) for i, j in beside]

    own_slice = split_slice(kernel_slices[0])
    partner = shift(own_slice, dz=1)
    first, second, inner = pack(after(density, own_slice), limiter)
    first = lax.ppermute(first, "space", beside)
    inner = shift(inner, dc=1)

    crossing = jnp.concatenate([partner[128:], own_slice[:128]], 0)
    cross = shift(crossing, dz=1, dh=1)
    first = after(first, crossing)
    second = lax.ppermute(after(second, first), "space", beside)
    block, own = transport_inner(density, limiter, heading, courant, first, inner)

    base = jnp.concatenate([own_slice[128:], partner[:128], after(cross, block)], 0)
    swapped = [shift(base, dc=1)]
    block = after(block, swapped[0])
    before, behind = shift(block, dy=1), shift(block, dy=-1)
    one, three, before, behind = after(
        (shift(base, dx=1), shift(base, dx=-1), before, behind)
    )
    pieces = [base, one, three, shift(one[:256], dx=1), shift(three[256:], dx=-1)]
    pieces = pieces + swapped + [shift(p, dc=1) for p in pieces[1:]]
    inside = [block, behind, before, shift(before[:64], dy=1), shift(behind[64:], dy=-1)]

    rows = after(jnp.concatenate([own, shift(own, dz=1)], 0), before)
    weights = [rows, shift(rows, dy=-1), shift(rows, dy=2), shift(rows, dy=1)]
    second = after(second, before)
    transported, block = transport(density, limiter, heading, courant, first, second, inner)
    before, behind = shift(block, dy=1), shift(block, dy=-1)
    across = shift(block, dy=2)
    outside = [block, behind, before, across[:64], across[64:]]

    waiting, result = [], None
    for layers, blocks in zip(BLOCKS, (inside, outside), strict=True):
        for place, layer in enumerate(layers):
            mine, other = collide(layer, place, pieces, blocks, weights)
            weights = after(weights, mine, *[got for _, _, got in waiting[:-1]])
            if waiting:
                result = combine(*waiting[-1][:2], after(waiting[-1][2], mine), result)
            waiting.append((layer, mine, shift(other, dz=1)))
    return transported, combine(*waiting[-1], result)


def solution(mesh):
    return jax.shard_map(
        local,
        mesh=mesh,
        in_specs=(
            P("vel", "space", None, None),
            P("space", None, None),
            P("vel"),
            P("vel"),
            P("space", None, "vel"),
        ),
        out_specs=(P("vel", "space", None, None), P("vel", "space", None, None)),
        check_vma=False,
    )
```

```python
import jax
import jax.numpy as jnp
from jax import lax
from jax.experimental import pallas as pl
from jax.experimental.pallas import tpu as pltpu
from jax.sharding import PartitionSpec as P

SLICES = 16
BLOCKS = ((1, 2), (0, 3))
BOTH = ("vel", "space")
FLAT = [
    (y, z, x, h, c)
    for y in range(4)
    for z in range(2)
    for x in range(4)
    for h in range(2)
    for c in range(2)
]
BF16, F32 = jnp.bfloat16, jnp.float32
ANY = pl.BlockSpec(memory_space=pl.ANY)
VMEM = pl.BlockSpec(memory_space=pltpu.VMEM)
SMEM = pl.BlockSpec(memory_space=pltpu.SMEM)


def rank(y, z, x, h, c):
    return ((y % 4) * 2 + z) * 16 + (x % 4) * 4 + h * 2 + c


def shift(value, dy=0, dz=0, dx=0, dh=0, dc=0):
    pairs = [
        (rank(y, z, x, h, c), rank(y + dy, z ^ dz, x + dx, h ^ dh, c ^ dc)) for y, z, x, h, c in FLAT
    ]
    return lax.ppermute(value, BOTH, pairs)


def after(value, *earlier):
    return lax.optimization_barrier((value, earlier))[0]


def shape(dims, dtype):
    return jax.ShapeDtypeStruct(dims, dtype)


def pack(density, limiter):
    rows = density.shape[0]

    def kernel(d_ref, l_ref, first_ref, second_ref, inner_ref):
        core = lax.axis_index("space") & 1

        def fill(outer, following, pair):
            first_ref[:rows] = d_ref[:, outer].astype(BF16)
            first_ref[rows] = l_ref[outer].astype(F32).astype(BF16)
            for i in range(2):
                first_ref[rows + 1 + i] = d_ref[64 * i, following].astype(BF16)
            second_ref[...] = d_ref[:, following].astype(BF16)
            inner_ref[:rows] = d_ref[:, pair : pair + 2].astype(BF16)
            inner_ref[rows] = l_ref[pair : pair + 2].astype(F32).astype(BF16)

        @pl.when(core == 1)
        def _():
            fill(3, 2, 0)

        @pl.when(core == 0)
        def _():
            fill(0, 1, 2)

    dims = density.shape[2:]
    return pl.pallas_call(
        kernel,
        out_shape=(
            shape((rows + 3, *dims), BF16),
            shape((rows, *dims), BF16),
            shape((rows + 1, 2, *dims), BF16),
        ),
        in_specs=[VMEM, VMEM],
        out_specs=(VMEM, VMEM, VMEM),
        name="pack",
    )(density, limiter)


def split_slice(kernel_slice):
    def kernel(k_ref, o_ref):
        z = lax.axis_index("vel") & 1
        for y in range(4):
            cols = pl.ds(y * 128, 128)
            o_ref[:128, cols] = k_ref[y, 1 - z].astype(F32).T.astype(BF16)
            o_ref[128:, cols] = k_ref[y, z].astype(F32).T.astype(BF16)

    return pl.pallas_call(
        kernel, out_shape=shape((256, 512), BF16), in_specs=[VMEM], out_specs=VMEM, name="split_slice"
    )(kernel_slice.reshape(4, 2, 128, 128))


def update(cells, codes, ahead, number, layers):
    half = 0.5 * (2 * ahead - 1).astype(F32)
    forward = jnp.full((8, 128), ahead, jnp.int32) == 1
    rebuilt = {}
    for i in sorted({i + d for i in layers for d in (-1, 0, 1)}):
        left, right = cells[i] - cells[i - 1], cells[i + 1] - cells[i]
        small = jnp.where(left > 0, jnp.minimum(left, right), jnp.maximum(left, right))
        small = jnp.where(left * right > 0, small, 0.0)
        slope = jnp.where(
            codes[i] == 1, small, jnp.where(codes[i] == 2, 0.5 * (left + right), 0.0)
        )
        rebuilt[i] = cells[i] + half * slope
    return [
        cells[i] - number * (rebuilt[i] - jnp.where(forward, rebuilt[i - 1], rebuilt[i + 1]))
        for i in layers
    ]


STEP = 32


def transport_specs(rows):
    return [
        SMEM,
        SMEM,
        pl.BlockSpec((STEP, 4, 8, 128), lambda i: (i, 0, 0, 0)),
        pl.BlockSpec((4, 8, 128), lambda i: (0, 0, 0)),
        pl.BlockSpec((STEP, 8, 128), lambda i: (i, 0, 0)),
        pl.BlockSpec((1, 8, 128), lambda i: (rows, 0, 0)),
        pl.BlockSpec((STEP, 2, 8, 128), lambda i: (i, 0, 0, 0)),
        pl.BlockSpec((1, 2, 8, 128), lambda i: (rows, 0, 0, 0)),
    ]


def outer_codes(core, l_ref, first_code, inner_code):
    codes = {i: l_ref[i].astype(F32) for i in range(4)}
    codes[-1] = jnp.where(core == 0, first_code[0].astype(F32), inner_code[0, 1].astype(F32))
    codes[4] = jnp.where(core == 0, inner_code[0, 0].astype(F32), first_code[0].astype(F32))
    return codes


def neighbours(core, j, first_ref, inner_ref, second=None):
    a, b = inner_ref[j, 0].astype(F32), inner_ref[j, 1].astype(F32)
    first = first_ref[j].astype(F32)
    cells = {-1: jnp.where(core == 0, first, b), 4: jnp.where(core == 0, a, first)}
    if second is not None:
        second = second.astype(F32)
        cells[-2] = jnp.where(core == 0, second, a)
        cells[5] = jnp.where(core == 0, b, second)
    return cells


def flatten(m_ref, t_ref, places):
    for place, i in enumerate(places):
        turned = jnp.swapaxes(t_ref[:, i], 0, 1)
        for y in range(8):
            m_ref[:, pl.ds(place * 1024 + y * 128, 128)] = turned[y].astype(BF16)


def transport_inner(density, limiter, heading, courant, first, inner):
    rows = density.shape[0]

    def kernel(
        h_ref, c_ref, d_ref, l_ref, first_ref, first_code, inner_ref, inner_code, next_ref, m_ref, w_ref, t_ref
    ):
        core = lax.axis_index("space") & 1
        start = pl.program_id(0) * STEP
        codes = outer_codes(core, l_ref, first_code, inner_code)

        def one(j, _):
            cells = {i: d_ref[j, i] for i in range(4)}
            cells.update(neighbours(core, j, first_ref, inner_ref))
            values = update(cells, codes, h_ref[start + j], c_ref[start + j], (1, 2))
            for i, value in enumerate(values):
                t_ref[j, i] = value
            return 0

        lax.fori_loop(0, STEP, one, 0, unroll=4)
        flatten(m_ref, t_ref, (0, 1))

        @pl.when(pl.program_id(0) % 2 == 0)
        def _():
            cells = {i: d_ref[0, i] for i in range(4)}
            cells.update(neighbours(core, 0, first_ref, inner_ref, next_ref[0]))
            values = update(cells, codes, h_ref[start], c_ref[start], range(4))
            for i, value in enumerate(values):
                w_ref[0, i] = value.astype(BF16)

    return pl.pallas_call(
        kernel,
        grid=(rows // STEP,),
        out_shape=(shape((rows, 2048), BF16), shape((2, 4, 8, 128), BF16)),
        in_specs=transport_specs(rows)
        + [pl.BlockSpec((1, 8, 128), lambda i: (rows + 1 + i // 2, 0, 0))],
        out_specs=(
            pl.BlockSpec((STEP, 2048), lambda i: (i, 0)),
            pl.BlockSpec((1, 4, 8, 128), lambda i: (i // 2, 0, 0, 0)),
        ),
        scratch_shapes=[pltpu.VMEM((STEP, 2, 8, 128), F32)],
        cost_estimate=pl.CostEstimate(flops=2 << 20, bytes_accessed=3 << 20, transcendentals=0),
        name="transport_inner",
    )(heading, courant, density, limiter, first, first, inner, inner, first)


def transport(density, limiter, heading, courant, first, second, inner):
    rows = density.shape[0]

    def kernel(
        h_ref, c_ref, d_ref, l_ref, first_ref, first_code, inner_ref, inner_code, next_ref, t_ref, m_ref
    ):
        core = lax.axis_index("space") & 1
        start = pl.program_id(0) * STEP
        codes = outer_codes(core, l_ref, first_code, inner_code)

        def one(j, _):
            cells = {i: d_ref[j, i] for i in range(4)}
            cells.update(neighbours(core, j, first_ref, inner_ref, next_ref[j]))
            values = update(cells, codes, h_ref[start + j], c_ref[start + j], range(4))
            for i, value in enumerate(values):
                t_ref[j, i] = value
            return 0

        lax.fori_loop(0, STEP, one, 0, unroll=4)
        flatten(m_ref, t_ref, (0, 3))

    return pl.pallas_call(
        kernel,
        grid=(rows // STEP,),
        out_shape=(shape(density.shape, F32), shape((rows, 2048), BF16)),
        in_specs=transport_specs(rows) + [pl.BlockSpec((STEP, 8, 128), lambda i: (i, 0, 0))],
        out_specs=(
            pl.BlockSpec((STEP, 4, 8, 128), lambda i: (i, 0, 0, 0)),
            pl.BlockSpec((STEP, 2048), lambda i: (i, 0)),
        ),
        cost_estimate=pl.CostEstimate(flops=4 << 20, bytes_accessed=6 << 20, transcendentals=0),
        name="transport",
    )(heading, courant, density, limiter, first, first, inner, inner, second)


ORDER = [(0, 0), (0, 1), (3, 0), (3, 1), (1, 0), (1, 1), (2, 0), (2, 1)]


def weight_rows():
    vel, space = lax.axis_index("vel"), lax.axis_index("space")
    y, z = vel >> 1, vel & 1
    x, h, c = space >> 2, (space >> 1) & 1, space & 1
    rows = []
    for dc in range(2):
        for dx, dh in ORDER:
            v = (((x + dx) & 3) << 1) + (h ^ dh)
            rows.append(((((v >> 1) - y) & 3) << 2) + (((v & 1) ^ z) << 1) + (c ^ dc))
    return y, rows


def collide(layer, place, pieces, blocks, weights):
    cells = 1024
    tile = 512
    columns = pl.ds(place * cells, cells)
    targets = [0, 1, 3, 2]

    def kernel(*refs):
        w_parts = refs[:4]
        slabs = refs[4:14]
        parts = refs[14:18]
        mine_ref, other_ref, k_ref, m_ref, w_ref, sem_k, sem_m = refs[18:]
        y, places = weight_rows()
        loads = []
        for i, d in enumerate(targets):
            at = pl.multiple_of(((y + d) & 3) * 128, 128)
            loads.append(
                pltpu.make_async_copy(
                    parts[i].at[:, columns], m_ref.at[pl.ds(at, 128)], sem_m.at[i]
                )
            )
        row, starts = 0, []
        for i in range(10):
            n = slabs[i].shape[0]
            loads.append(pltpu.make_async_copy(slabs[i], k_ref.at[pl.ds(row, n)], sem_k.at[i]))
            starts.append(row // 256)
            row += n
        for load in loads:
            load.start()
        for d in range(4):
            w_ref[4 * d : 4 * d + 4] = w_parts[d][:, layer].astype(F32)
        for load in loads[:4]:
            load.wait()
        for t in range(cells // tile):
            cols = pl.ds(t * tile, tile)
            moved = m_ref[:, cols]
            total = jnp.zeros((256, tile), F32)
            for s in range(SLICES):
                if t == 0 and s in starts:
                    loads[4 + starts.index(s)].wait()
                product = jnp.dot(
                    k_ref[s * 256 : (s + 1) * 256], moved, preferred_element_type=F32
                )
                lines = [w_ref[places[s], pl.ds(t * 4 + i, 1), :] for i in range(tile // 128)]
                total = total + jnp.concatenate(lines, 1) * product
            mine_ref[:, cols] = total[:128]
            other_ref[:, cols] = total[128:].astype(BF16)

    return pl.pallas_call(
        kernel,
        out_shape=(shape((128, cells), F32), shape((128, cells), BF16)),
        in_specs=[VMEM] * 4 + [ANY] * 14,
        out_specs=(VMEM, VMEM),
        scratch_shapes=[
            pltpu.VMEM((SLICES * 256, 512), BF16),
            pltpu.VMEM((512, cells), BF16),
            pltpu.VMEM((SLICES, 8, 128), F32),
            pltpu.SemaphoreType.DMA((10,)),
            pltpu.SemaphoreType.DMA((4,)),
        ],
        compiler_params=pltpu.CompilerParams(vmem_limit_bytes=28 << 20),
        cost_estimate=pl.CostEstimate(
            flops=2 * SLICES * 256 * 512 * cells, bytes_accessed=6 << 20, transcendentals=0
        ),
        name="collide",
    )(*weights, *pieces, *blocks)


def combine(layer, mine, got, result):
    step = 64

    def kernel(a_ref, b_ref, *refs):
        o_ref = refs[-1]
        total = a_ref[...] + b_ref[...].astype(F32)
        lines = jnp.stack([total[:, y * 128 : (y + 1) * 128] for y in range(8)], 0)
        o_ref[:, 0] = jnp.swapaxes(lines, 0, 1)

    block = pl.BlockSpec((step, 1024), lambda i: (i, 0))
    given = [] if result is None else [result]
    return pl.pallas_call(
        kernel,
        grid=(128 // step,),
        out_shape=shape((128, 4, 8, 128), F32),
        in_specs=[block, block] + [ANY] * len(given),
        out_specs=pl.BlockSpec((step, 1, 8, 128), lambda i: (i, layer, 0, 0)),
        input_output_aliases={2: 0} if given else {},
        cost_estimate=pl.CostEstimate(flops=1 << 17, bytes_accessed=5 << 18, transcendentals=0),
        name="combine",
    )(mine, got, *given)


def local(density, limiter, heading, courant, kernel_slices):
    size = lax.axis_size("space")
    beside = [(i, i + 1) for i in range(1, size - 1, 2)]
    beside = beside + [(j, i) for i, j in beside]

    own_slice = split_slice(kernel_slices[0])
    partner = shift(own_slice, dz=1)
    first, second, inner = pack(after(density, own_slice), limiter)
    first = lax.ppermute(first, "space", beside)
    inner = shift(inner, dc=1)

    crossing = jnp.concatenate([partner[128:], own_slice[:128]], 0)
    cross = shift(crossing, dz=1, dh=1)
    first = after(first, crossing)
    second = lax.ppermute(after(second, first), "space", beside)
    block, own = transport_inner(density, limiter, heading, courant, first, inner)

    base = jnp.concatenate([own_slice[128:], partner[:128], after(cross, block)], 0)
    swapped = [shift(base, dc=1)]
    block = after(block, swapped[0])
    before, behind, across = shift(block, dy=1), shift(block, dy=-1), shift(block, dy=2)
    one, three, before, behind = after(
        (shift(base, dx=1), shift(base, dx=-1), before, behind)
    )
    pieces = [base, one, three, shift(one[:256], dx=1), shift(three[256:], dx=-1)]
    pieces = pieces + swapped + [shift(p, dc=1) for p in pieces[1:]]
    inside = [block, behind, before, across]

    rows = after(jnp.concatenate([own, shift(own, dz=1)], 0), before)
    weights = [rows, shift(rows, dy=-1), shift(rows, dy=2), shift(rows, dy=1)]
    second = after(second, before)
    transported, block = transport(density, limiter, heading, courant, first, second, inner)
    before, behind = shift(block, dy=1), shift(block, dy=-1)
    across = shift(block, dy=2)
    outside = [block, behind, before, across]

    waiting, result = [], None
    for layers, blocks in zip(BLOCKS, (inside, outside), strict=True):
        for place, layer in enumerate(layers):
            mine, other = collide(layer, place, pieces, blocks, weights)
            weights = after(weights, mine, *[got for _, _, got in waiting[:-1]])
            if waiting:
                result = combine(*waiting[-1][:2], after(waiting[-1][2], mine), result)
            waiting.append((layer, mine, shift(other, dz=1)))
    return transported, combine(*waiting[-1], result)


def solution(mesh):
    return jax.shard_map(
        local,
        mesh=mesh,
        in_specs=(
            P("vel", "space", None, None),
            P("space", None, None),
            P("vel"),
            P("vel"),
            P("space", None, "vel"),
        ),
        out_specs=(P("vel", "space", None, None), P("vel", "space", None, None)),
        check_vma=False,
    )
```

```python
import jax
import jax.numpy as jnp
from jax import lax
from jax.experimental import pallas as pl
from jax.experimental.pallas import tpu as pltpu
from jax.sharding import PartitionSpec as P

SLICES = 16
BLOCKS = ((1, 2), (0, 3))
BOTH = ("vel", "space")
FLAT = [
    (y, z, x, h, c)
    for y in range(4)
    for z in range(2)
    for x in range(4)
    for h in range(2)
    for c in range(2)
]
BF16, F32 = jnp.bfloat16, jnp.float32
ANY = pl.BlockSpec(memory_space=pl.ANY)
VMEM = pl.BlockSpec(memory_space=pltpu.VMEM)
SMEM = pl.BlockSpec(memory_space=pltpu.SMEM)


def rank(y, z, x, h, c):
    return ((y % 4) * 2 + z) * 16 + (x % 4) * 4 + h * 2 + c


def shift(value, dy=0, dz=0, dx=0, dh=0, dc=0):
    pairs = [
        (rank(y, z, x, h, c), rank(y + dy, z ^ dz, x + dx, h ^ dh, c ^ dc)) for y, z, x, h, c in FLAT
    ]
    return lax.ppermute(value, BOTH, pairs)


def after(value, *earlier):
    return lax.optimization_barrier((value, earlier))[0]


def shape(dims, dtype):
    return jax.ShapeDtypeStruct(dims, dtype)


def pack(density, limiter):
    rows = density.shape[0]

    def kernel(d_ref, l_ref, first_ref, second_ref, inner_ref):
        core = lax.axis_index("space") & 1

        def fill(outer, following, pair):
            first_ref[:rows] = d_ref[:, outer].astype(BF16)
            first_ref[rows] = l_ref[outer].astype(F32).astype(BF16)
            for i in range(2):
                first_ref[rows + 1 + i] = d_ref[64 * i, following].astype(BF16)
            second_ref[...] = d_ref[:, following].astype(BF16)
            inner_ref[:rows] = d_ref[:, pair : pair + 2].astype(BF16)
            inner_ref[rows] = l_ref[pair : pair + 2].astype(F32).astype(BF16)

        @pl.when(core == 1)
        def _():
            fill(3, 2, 0)

        @pl.when(core == 0)
        def _():
            fill(0, 1, 2)

    dims = density.shape[2:]
    return pl.pallas_call(
        kernel,
        out_shape=(
            shape((rows + 3, *dims), BF16),
            shape((rows, *dims), BF16),
            shape((rows + 1, 2, *dims), BF16),
        ),
        in_specs=[VMEM, VMEM],
        out_specs=(VMEM, VMEM, VMEM),
        name="pack",
    )(density, limiter)


def split_slice(kernel_slice):
    def kernel(k_ref, o_ref):
        z = lax.axis_index("vel") & 1
        for y in range(4):
            cols = pl.ds(y * 128, 128)
            o_ref[:128, cols] = k_ref[y, 1 - z].astype(F32).T.astype(BF16)
            o_ref[128:, cols] = k_ref[y, z].astype(F32).T.astype(BF16)

    return pl.pallas_call(
        kernel, out_shape=shape((256, 512), BF16), in_specs=[VMEM], out_specs=VMEM, name="split_slice"
    )(kernel_slice.reshape(4, 2, 128, 128))


def update(cells, codes, ahead, number, layers):
    half = 0.5 * (2 * ahead - 1).astype(F32)
    forward = jnp.full((8, 128), ahead, jnp.int32) == 1
    rebuilt = {}
    for i in sorted({i + d for i in layers for d in (-1, 0, 1)}):
        left, right = cells[i] - cells[i - 1], cells[i + 1] - cells[i]
        small = jnp.where(left > 0, jnp.minimum(left, right), jnp.maximum(left, right))
        small = jnp.where(left * right > 0, small, 0.0)
        slope = jnp.where(
            codes[i] == 1, small, jnp.where(codes[i] == 2, 0.5 * (left + right), 0.0)
        )
        rebuilt[i] = cells[i] + half * slope
    return [
        cells[i] - number * (rebuilt[i] - jnp.where(forward, rebuilt[i - 1], rebuilt[i + 1]))
        for i in layers
    ]


STEP = 32


def transport_specs(rows):
    return [
        SMEM,
        SMEM,
        pl.BlockSpec((STEP, 4, 8, 128), lambda i: (i, 0, 0, 0)),
        pl.BlockSpec((4, 8, 128), lambda i: (0, 0, 0)),
        pl.BlockSpec((STEP, 8, 128), lambda i: (i, 0, 0)),
        pl.BlockSpec((1, 8, 128), lambda i: (rows, 0, 0)),
        pl.BlockSpec((STEP, 2, 8, 128), lambda i: (i, 0, 0, 0)),
        pl.BlockSpec((1, 2, 8, 128), lambda i: (rows, 0, 0, 0)),
    ]


def outer_codes(core, l_ref, first_code, inner_code):
    codes = {i: l_ref[i].astype(F32) for i in range(4)}
    codes[-1] = jnp.where(core == 0, first_code[0].astype(F32), inner_code[0, 1].astype(F32))
    codes[4] = jnp.where(core == 0, inner_code[0, 0].astype(F32), first_code[0].astype(F32))
    return codes


def neighbours(core, j, first_ref, inner_ref, second=None):
    a, b = inner_ref[j, 0].astype(F32), inner_ref[j, 1].astype(F32)
    first = first_ref[j].astype(F32)
    cells = {-1: jnp.where(core == 0, first, b), 4: jnp.where(core == 0, a, first)}
    if second is not None:
        second = second.astype(F32)
        cells[-2] = jnp.where(core == 0, second, a)
        cells[5] = jnp.where(core == 0, b, second)
    return cells


def flatten(m_ref, t_ref, places):
    for place, i in enumerate(places):
        turned = jnp.swapaxes(t_ref[:, i], 0, 1)
        for y in range(8):
            m_ref[:, pl.ds(place * 1024 + y * 128, 128)] = turned[y].astype(BF16)


def transport_inner(density, limiter, heading, courant, first, inner):
    rows = density.shape[0]

    def kernel(
        h_ref, c_ref, d_ref, l_ref, first_ref, first_code, inner_ref, inner_code, next_ref, m_ref, w_ref, t_ref
    ):
        core = lax.axis_index("space") & 1
        start = pl.program_id(0) * STEP
        codes = outer_codes(core, l_ref, first_code, inner_code)

        def one(j, _):
            cells = {i: d_ref[j, i] for i in range(4)}
            cells.update(neighbours(core, j, first_ref, inner_ref))
            values = update(cells, codes, h_ref[start + j], c_ref[start + j], (1, 2))
            for i, value in enumerate(values):
                t_ref[j, i] = value
            return 0

        lax.fori_loop(0, STEP, one, 0, unroll=4)
        flatten(m_ref, t_ref, (0, 1))

        @pl.when(pl.program_id(0) % 2 == 0)
        def _():
            cells = {i: d_ref[0, i] for i in range(4)}
            cells.update(neighbours(core, 0, first_ref, inner_ref, next_ref[0]))
            values = update(cells, codes, h_ref[start], c_ref[start], range(4))
            for i, value in enumerate(values):
                w_ref[0, i] = value.astype(BF16)

    return pl.pallas_call(
        kernel,
        grid=(rows // STEP,),
        out_shape=(shape((rows, 2048), BF16), shape((2, 4, 8, 128), BF16)),
        in_specs=transport_specs(rows)
        + [pl.BlockSpec((1, 8, 128), lambda i: (rows + 1 + i // 2, 0, 0))],
        out_specs=(
            pl.BlockSpec((STEP, 2048), lambda i: (i, 0)),
            pl.BlockSpec((1, 4, 8, 128), lambda i: (i // 2, 0, 0, 0)),
        ),
        scratch_shapes=[pltpu.VMEM((STEP, 2, 8, 128), F32)],
        cost_estimate=pl.CostEstimate(flops=2 << 20, bytes_accessed=3 << 20, transcendentals=0),
        name="transport_inner",
    )(heading, courant, density, limiter, first, first, inner, inner, first)


def transport(density, limiter, heading, courant, first, second, inner):
    rows = density.shape[0]

    def kernel(
        h_ref, c_ref, d_ref, l_ref, first_ref, first_code, inner_ref, inner_code, next_ref, t_ref, m_ref
    ):
        core = lax.axis_index("space") & 1
        start = pl.program_id(0) * STEP
        codes = outer_codes(core, l_ref, first_code, inner_code)

        def one(j, _):
            cells = {i: d_ref[j, i] for i in range(4)}
            cells.update(neighbours(core, j, first_ref, inner_ref, next_ref[j]))
            values = update(cells, codes, h_ref[start + j], c_ref[start + j], range(4))
            for i, value in enumerate(values):
                t_ref[j, i] = value
            return 0

        lax.fori_loop(0, STEP, one, 0, unroll=4)
        flatten(m_ref, t_ref, (0, 3))

    return pl.pallas_call(
        kernel,
        grid=(rows // STEP,),
        out_shape=(shape(density.shape, F32), shape((rows, 2048), BF16)),
        in_specs=transport_specs(rows) + [pl.BlockSpec((STEP, 8, 128), lambda i: (i, 0, 0))],
        out_specs=(
            pl.BlockSpec((STEP, 4, 8, 128), lambda i: (i, 0, 0, 0)),
            pl.BlockSpec((STEP, 2048), lambda i: (i, 0)),
        ),
        cost_estimate=pl.CostEstimate(flops=4 << 20, bytes_accessed=6 << 20, transcendentals=0),
        name="transport",
    )(heading, courant, density, limiter, first, first, inner, inner, second)


ORDER = [(0, 0), (0, 1), (3, 0), (3, 1), (1, 0), (1, 1), (2, 0), (2, 1)]


def weight_rows():
    vel, space = lax.axis_index("vel"), lax.axis_index("space")
    y, z = vel >> 1, vel & 1
    x, h, c = space >> 2, (space >> 1) & 1, space & 1
    rows = []
    for dc in range(2):
        for dx, dh in ORDER:
            v = (((x + dx) & 3) << 1) + (h ^ dh)
            rows.append(((((v >> 1) - y) & 3) << 2) + (((v & 1) ^ z) << 1) + (c ^ dc))
    return y, rows


def collide(layer, place, pieces, blocks, weights):
    cells = 1024
    tile = 512
    columns = pl.ds(place * cells, cells)
    targets = [(0, 0, 128), (1, 0, 128), (3, 0, 128), (2, 0, 64), (2, 64, 64)]

    def kernel(*refs):
        w_parts = refs[:4]
        slabs = refs[4:14]
        parts = refs[14:19]
        mine_ref, other_ref, k_ref, m_ref, w_ref, sem_k, sem_m = refs[19:]
        y, places = weight_rows()
        loads = []
        for i, (d, skip, n) in enumerate(targets):
            at = pl.multiple_of(((y + d) & 3) * 128 + skip, 64)
            loads.append(
                pltpu.make_async_copy(
                    parts[i].at[:, columns], m_ref.at[pl.ds(at, n)], sem_m.at[i]
                )
            )
        row, starts = 0, []
        for i in range(10):
            n = slabs[i].shape[0]
            loads.append(pltpu.make_async_copy(slabs[i], k_ref.at[pl.ds(row, n)], sem_k.at[i]))
            starts.append(row // 256)
            row += n
        for load in loads:
            load.start()
        for d in range(4):
            w_ref[4 * d : 4 * d + 4] = w_parts[d][:, layer].astype(F32)
        for load in loads[:5]:
            load.wait()
        for t in range(cells // tile):
            cols = pl.ds(t * tile, tile)
            moved = m_ref[:, cols]
            total = jnp.zeros((256, tile), F32)
            for s in range(SLICES):
                if t == 0 and s in starts:
                    loads[5 + starts.index(s)].wait()
                product = jnp.dot(
                    k_ref[s * 256 : (s + 1) * 256], moved, preferred_element_type=F32
                )
                lines = [w_ref[places[s], pl.ds(t * 4 + i, 1), :] for i in range(tile // 128)]
                total = total + jnp.concatenate(lines, 1) * product
            mine_ref[:, cols] = total[:128].astype(BF16)
            other_ref[:, cols] = total[128:].astype(BF16)

    return pl.pallas_call(
        kernel,
        out_shape=(shape((128, cells), BF16), shape((128, cells), BF16)),
        in_specs=[VMEM] * 4 + [ANY] * 15,
        out_specs=(VMEM, VMEM),
        scratch_shapes=[
            pltpu.VMEM((SLICES * 256, 512), BF16),
            pltpu.VMEM((512, cells), BF16),
            pltpu.VMEM((SLICES, 8, 128), F32),
            pltpu.SemaphoreType.DMA((10,)),
            pltpu.SemaphoreType.DMA((5,)),
        ],
        compiler_params=pltpu.CompilerParams(vmem_limit_bytes=28 << 20),
        cost_estimate=pl.CostEstimate(
            flops=2 * SLICES * 256 * 512 * cells, bytes_accessed=6 << 20, transcendentals=0
        ),
        name="collide",
    )(*weights, *pieces, *blocks)


def combine(layer, mine, got, result):
    step = 64

    def kernel(a_ref, b_ref, *refs):
        o_ref = refs[-1]
        total = a_ref[...].astype(F32) + b_ref[...].astype(F32)
        lines = jnp.stack([total[:, y * 128 : (y + 1) * 128] for y in range(8)], 0)
        o_ref[:, 0] = jnp.swapaxes(lines, 0, 1)

    block = pl.BlockSpec((step, 1024), lambda i: (i, 0))
    given = [] if result is None else [result]
    return pl.pallas_call(
        kernel,
        grid=(128 // step,),
        out_shape=shape((128, 4, 8, 128), F32),
        in_specs=[block, block] + [ANY] * len(given),
        out_specs=pl.BlockSpec((step, 1, 8, 128), lambda i: (i, layer, 0, 0)),
        input_output_aliases={2: 0} if given else {},
        cost_estimate=pl.CostEstimate(flops=1 << 17, bytes_accessed=5 << 18, transcendentals=0),
        name="combine",
    )(mine, got, *given)


def local(density, limiter, heading, courant, kernel_slices):
    size = lax.axis_size("space")
    beside = [(i, i + 1) for i in range(1, size - 1, 2)]
    beside = beside + [(j, i) for i, j in beside]

    own_slice = split_slice(kernel_slices[0])
    partner = shift(own_slice, dz=1)
    first, second, inner = pack(after(density, own_slice), limiter)
    first = lax.ppermute(first, "space", beside)
    inner = shift(inner, dc=1)

    crossing = jnp.concatenate([partner[128:], own_slice[:128]], 0)
    cross = shift(crossing, dz=1, dh=1)
    first = after(first, crossing)
    second = lax.ppermute(after(second, first), "space", beside)
    block, own = transport_inner(density, limiter, heading, courant, first, inner)

    base = jnp.concatenate([own_slice[128:], partner[:128], after(cross, block)], 0)
    swapped = [shift(base, dc=1)]
    block = after(block, swapped[0])
    before, behind = shift(block, dy=1), shift(block, dy=-1)
    one, three, before, behind = after(
        (shift(base, dx=1), shift(base, dx=-1), before, behind)
    )
    pieces = [base, one, three, shift(one[:256], dx=1), shift(three[256:], dx=-1)]
    pieces = pieces + swapped + [shift(p, dc=1) for p in pieces[1:]]
    inside = [block, behind, before, shift(before[:64], dy=1), shift(behind[64:], dy=-1)]

    rows = after(jnp.concatenate([own, shift(own, dz=1)], 0), before)
    weights = [rows, shift(rows, dy=-1), shift(rows, dy=2), shift(rows, dy=1)]
    second = after(second, before)
    transported, block = transport(density, limiter, heading, courant, first, second, inner)
    before, behind = shift(block, dy=1), shift(block, dy=-1)
    across = shift(block, dy=2)
    outside = [block, behind, before, across[:64], across[64:]]

    waiting, result = [], None
    for layers, blocks in zip(BLOCKS, (inside, outside), strict=True):
        for place, layer in enumerate(layers):
            mine, other = collide(layer, place, pieces, blocks, weights)
            weights = after(weights, mine, *[got for _, _, got in waiting[:-1]])
            if waiting:
                result = combine(*waiting[-1][:2], after(waiting[-1][2], mine), result)
            waiting.append((layer, mine, shift(other, dz=1)))
    return transported, combine(*waiting[-1], result)


def solution(mesh):
    return jax.shard_map(
        local,
        mesh=mesh,
        in_specs=(
            P("vel", "space", None, None),
            P("space", None, None),
            P("vel"),
            P("vel"),
            P("space", None, "vel"),
        ),
        out_specs=(P("vel", "space", None, None), P("vel", "space", None, None)),
        check_vma=False,
    )
```
